256 devices in a mesh: col: 4 (over z_lo), grp: 64 (over x, z_hi, y, core).
Axes of the slice: x: 4, y: 4, z: 8 (z_hi: 2, z_lo: 4; z = z_hi * 4 + z_lo), core: 2. Of those that a mesh axis runs over, the one named last changes fastest.
Arguments:
- table_rows: bfloat16 [64, 256, 256], P('grp', None, 'col'), may hold values from -1.5 to 1.5
- pool_index: int32 [64, 4, 8192], P('grp'), may hold values from 0 to 255
- bag_length: int32 [64, 8192], P('grp'), may hold values from 1 to 4
- table_slot: int32 [64], replicated, may hold values from 0 to 63, each once
- dense_input: bfloat16 [8192, 13], P('grp'), may hold values from -6 to 6
- bottom_weight: bfloat16 [13, 256], replicated, may hold values from -1.75 to 1.75
- top_weight: bfloat16 [2336, 2048], P(None, 'col'), may hold values from -0.125 to 0.125
- out_weight: bfloat16 [2048], P('col'), may hold values from -0.125 to 0.125
- labels: int32 [8192], P('grp'), may hold values 0 or 1
Outputs:
- logits: float32 [8192], P('grp')
- grad_top: float32 [2336, 2048], P(None, ('col', 'grp'))
- grad_out: float32 [2048], P(('col', 'grp'))
- grad_bottom: float32 [13, 256], replicated
- grad_rows: float32 [64, 256, 256], P('grp', None, 'col')
The draws below stay inside these ranges and needn't reach their ends.
Inputs may be any that keep to these rules, and one draw needn't show every extreme that they name: `pool_index`: each entry names one of its table's 256 looked-up rows. `bag_length`: slots at or past a bag's length are unused. `table_slot`: every feature is held by exactly one shard.
All inputs are finite; a program needn't handle non-finite values. No bound on the sum of `labels` on one device may be relied on, other than what follows from the above.
Results may differ from the reference program's by a relative error of at most 0.0071.
Values may be sent and summed in bfloat16 or wider, within the bound.
No kernel may reach another device: no remote copies, remote signals or barrier semaphores. Data moves between devices by JAX's collectives and lax.ppermute only.
A program may use at most 128 MiB of HBM per device.

```python
import math
import jax
import jax.numpy as jnp
import numpy as np
from jax import lax

D_EMB = 256
HID = 2048
DENSE = 13
BAG = 4
UNIQ = 256
SAMP_DEV = 128
TABLES = 64
SAMPLES = 8192
TOPIN = 2336


def with_ends(drawn, own_key, least, largest):
    longest = drawn.shape.index(max(drawn.shape))
    spots = []
    for shift in (0, 1):
        where = [jax.random.randint(jax.random.fold_in(own_key, axis), (), 0, length) for axis, length in enumerate(drawn.shape)]
        where[longest] = (where[longest] + shift) % drawn.shape[longest]
        spots.append(tuple(where))
    return drawn.at[spots[0]].set(least).at[spots[1]].set(largest)


def block_levels(own_key, extent, shards, least, high):
    loudness = 1.0
    for dim, blocks in shards:
        heights = jax.random.uniform(jax.random.fold_in(jax.random.fold_in(own_key, 6), dim), (blocks,), jnp.float32, least / len(shards), high / len(shards))
        loudness = loudness * jnp.repeat(jnp.exp(heights), extent[dim] // blocks).reshape((-1,) + (1,) * (len(extent) - 1 - dim))
    return loudness


def cumulative_ranks(number_of, lean):
    portions = [(1 << 20) // math.isqrt(rank ** lean) + 1 for rank in range(1, number_of + 1)]
    spread = 1 + sum(portions) // (1 << 30)
    return np.cumsum(np.array([max(1, weight // spread) for weight in portions]))


def ranked(own_key, dims, count, skew):
    table = cumulative_ranks(count, skew)
    ticket = jax.random.randint(jax.random.fold_in(own_key, 1), dims, 0, int(table[count - 1]))
    standing = jnp.searchsorted(jnp.asarray(table, jnp.int32), ticket, side="right")
    return jax.random.permutation(jax.random.fold_in(own_key, 2), count)[standing].astype(jnp.int32)


def normal_values(rng, dims, width, limit, shards=(), dtype=jnp.bfloat16):
    gain = block_levels(rng, dims, shards, -0.22, 0.18) if shards else 1.0
    entries = jax.random.normal(rng, dims, jnp.float32) * width * gain
    return jnp.minimum(jnp.maximum(entries, -limit), limit).astype(dtype)


def setup_inputs(seed: int = 0) -> dict:
    seeds = jax.random.split(jax.random.key(seed), 10)
    return {
        "table_rows": normal_values(seeds[0], (TABLES, UNIQ, D_EMB), 0.25, 1.5, ((0, 64), (2, 4))),
        "pool_index": with_ends(ranked(seeds[1], (TABLES, BAG, SAMPLES), UNIQ, 2), jax.random.fold_in(seeds[1], 3), 0, UNIQ - 1).astype(jnp.int32),
        "bag_length": with_ends(jax.random.randint(seeds[2], (TABLES, SAMPLES), 1, BAG + 1), jax.random.fold_in(seeds[2], 1), 1, BAG).astype(jnp.int32),
        "table_slot": jax.random.permutation(seeds[3], TABLES).astype(jnp.int32),
        "dense_input": normal_values(seeds[4], (SAMPLES, DENSE), 1.0, 6.0, ((0, 64),)),
        "bottom_weight": normal_values(seeds[5], (DENSE, D_EMB), DENSE ** -0.5, 1.75),
        "top_weight": normal_values(seeds[6], (TOPIN, HID), TOPIN ** -0.5, 0.125, ((1, 4),)),
        "out_weight": normal_values(seeds[7], (HID,), HID ** -0.5, 0.125, ((0, 4),)),
        "labels": with_ends((jax.random.randint(seeds[8], (SAMPLES,), 0, 2) < 1).astype(jnp.int32), jax.random.fold_in(seeds[8], 1), 0, 1),
    }


def pair_table(fields):
    upper_a, upper_b = np.triu_indices(fields, 1)
    return upper_a * fields + upper_b


def silu_slope(values):
    sigma = jax.nn.sigmoid(values)
    return sigma * (1.0 + values * (1.0 - sigma))


def reference(table_rows, pool_index, bag_length, table_slot, dense_input, bottom_weight, top_weight, out_weight, labels):
    def pool_one(inputs):
        table_block, index_block, length_block = inputs
        active = (lax.broadcasted_iota(jnp.int32, index_block.shape, 0) < length_block[None, :]).astype(jnp.float32)
        picked = table_block.astype(jnp.float32)[index_block]
        return jnp.sum(picked * active[:, :, None], axis=0).astype(jnp.bfloat16)

    pooled = lax.map(pool_one, (table_rows, pool_index, bag_length))
    bottom_pre = jnp.dot(dense_input, bottom_weight, preferred_element_type=jnp.float32)
    bottom_out = jax.nn.silu(bottom_pre).astype(jnp.bfloat16)
    inverse = jnp.argsort(table_slot).astype(jnp.int32)
    vectors = jnp.concatenate([bottom_out[None], jnp.take(pooled, inverse, axis=0)], axis=0)
    fields = vectors.shape[0]
    pair_flat = pair_table(fields)
    wide_vectors = vectors.astype(jnp.float32)
    gram_matrix = jnp.einsum("asc,bsc->abs", wide_vectors, wide_vectors)
    pair_values = gram_matrix.reshape(fields * fields, -1)[pair_flat]
    features = jnp.concatenate([bottom_out.astype(jnp.float32), pair_values.T], axis=1).astype(jnp.bfloat16)
    hidden_pre = jnp.dot(features, top_weight, preferred_element_type=jnp.float32)
    hidden = jax.nn.silu(hidden_pre).astype(jnp.bfloat16)
    logits = jnp.dot(hidden, out_weight, preferred_element_type=jnp.float32)
    dlogit = (jax.nn.sigmoid(logits) - labels.astype(jnp.float32)) / SAMP_DEV
    grad_out = jnp.dot(hidden.astype(jnp.float32).T, dlogit, precision=lax.Precision.HIGHEST)
    out_delta = (dlogit[:, None] * out_weight.astype(jnp.float32)[None, :] * silu_slope(hidden_pre)).astype(jnp.bfloat16)
    grad_top = jnp.dot(features.T, out_delta, preferred_element_type=jnp.float32)
    dfeatures = jnp.dot(out_delta, top_weight.T, preferred_element_type=jnp.float32)
    dpairs = dfeatures[:, D_EMB:].astype(jnp.bfloat16)
    symmetric = jnp.zeros((fields * fields, dpairs.shape[0]), jnp.bfloat16).at[pair_flat].set(dpairs.T)
    symmetric = symmetric.reshape(fields, fields, -1)
    symmetric = symmetric + jnp.transpose(symmetric, (1, 0, 2))
    dvectors = jnp.einsum("abs,bsc->asc", symmetric.astype(jnp.float32), wide_vectors)
    dbottom = (dfeatures[:, :D_EMB] + dvectors[0]) * silu_slope(bottom_pre)
    grad_bottom = jnp.dot(dense_input.astype(jnp.float32).T, dbottom, precision=lax.Precision.HIGHEST)
    dpooled = jnp.take(dvectors[1:], table_slot, axis=0).astype(jnp.bfloat16)

    def grads_one(inputs):
        index_block, length_block, grad_block = inputs
        active = lax.broadcasted_iota(jnp.int32, index_block.shape, 0) < length_block[None, :]
        row_ids = jnp.where(active, index_block, 0).reshape(-1)
        weights = active.astype(jnp.float32)[:, :, None] * grad_block.astype(jnp.float32)[None]
        return jax.ops.segment_sum(weights.reshape(-1, weights.shape[2]), row_ids, num_segments=UNIQ)

    grad_rows = lax.map(grads_one, (pool_index, bag_length, dpooled))
    return logits, grad_top, grad_out, grad_bottom, grad_rows
```

```python
import jax
import jax.numpy as jnp
import numpy as np
from jax import lax
from jax.experimental import pallas as pl
from jax.experimental.pallas import tpu as pltpu
from jax.sharding import Mesh
from jax.sharding import PartitionSpec as P

COL_GRP = ("col", "grp_0", "grp_1", "grp_2", "grp_3")
GRP = ("grp_0", "grp_1", "grp_2", "grp_3")
F32 = jnp.float32
BF16 = jnp.bfloat16

TAB = 64
ROWS = 16
LANES = 128
HALF = 64
EMB = 256
FEAT = 2336
WIDE = 2432
STEP = 8


def pieces():
    found = [(-1, 0, TAB, EMB)]
    place = EMB + TAB
    for row in range(TAB - 1):
        found.append((row, row + 1, TAB - 1 - row, place))
        place += TAB - 1 - row
    return found


def parts_of(place, count):
    found = []
    for tile in range(place // LANES, (place + count - 1) // LANES + 1):
        first = max(place, tile * LANES) - tile * LANES
        end = min(place + count, (tile + 1) * LANES) - tile * LANES
        found.append((tile, first, end))
    return found


def lane_iota(rows):
    return lax.broadcasted_iota(jnp.int32, (rows, LANES), 1)


def low_lanes(rows):
    return lane_iota(rows) < HALF


def turned(x, shift):
    shift %= LANES
    return x if shift == 0 else pltpu.roll(x, shift, 1)


def dot_t(a, b):
    return lax.dot_general(a, b, (((1,), (1,)), ((), ())), preferred_element_type=F32)


def pool_kernel(index_ref, length_ref, rows_ref, out_ref, weights, counted):
    @pl.when(pl.program_id(0) == 0)
    def _():
        weights[...] = jnp.zeros_like(weights)
        weights[0:HALF, 0:256] = rows_ref[0]
        weights[HALF:LANES, 256:512] = rows_ref[0]

    values = lax.broadcasted_iota(jnp.int32, (LANES, 256), 1)
    slots = lax.broadcasted_iota(jnp.int32, (8, LANES), 0)
    for group in range(STEP):
        lanes = slice(group * LANES, (group + 1) * LANES)
        index = index_ref[0, :, lanes]
        index = jnp.concatenate([index, index], axis=0)
        ids = jnp.where(slots < length_ref[0:1, lanes], index, -1).T
        counts = jnp.zeros((LANES, 256), F32)
        for slot in range(4):
            counts = counts + jnp.where(ids[:, slot : slot + 1] == values, 1.0, 0.0)
        counts = counts.astype(BF16)
        counted[group * HALF : (group + 1) * HALF, 0:256] = counts[0:HALF]
        counted[group * HALF : (group + 1) * HALF, 256:512] = counts[HALF:LANES]
    pooled = dot_t(counted[...], weights[...]).astype(BF16)
    for group in range(STEP):
        for peer in range(4):
            first = group * HALF + peer * ROWS
            out_ref[peer, group] = pooled[first : first + ROWS]


def pool(pool_index, bag_length, rows):
    return pl.pallas_call(
        pool_kernel,
        grid=(TAB // STEP,),
        in_specs=[
            pl.BlockSpec((1, 4, STEP * LANES), lambda i: (0, 0, i)),
            pl.BlockSpec((1, STEP * LANES), lambda i: (0, i)),
            pl.BlockSpec((1, HALF, 256), lambda i: (0, 0, 0)),
        ],
        out_specs=pl.BlockSpec((4, STEP, ROWS, LANES), lambda i: (0, i, 0, 0)),
        out_shape=jax.ShapeDtypeStruct((4, TAB, ROWS, LANES), BF16),
        scratch_shapes=[
            pltpu.VMEM((LANES, 512), BF16),
            pltpu.VMEM((STEP * HALF, 512), BF16),
        ],
        compiler_params=pltpu.CompilerParams(vmem_limit_bytes=12 << 20),
        name="pool",
    )(pool_index, bag_length, rows)


def packed_bottom(mine_ref):
    low = low_lanes(ROWS)
    tiles = []
    for pair in range(2):
        lanes = slice(pair * LANES, (pair + 1) * LANES)
        first, second = mine_ref[0:ROWS, lanes], mine_ref[ROWS : 2 * ROWS, lanes]
        tiles.append(jnp.where(low, first, turned(second, HALF)))
        tiles.append(jnp.where(low, turned(first, HALF), second))
    return jnp.concatenate(tiles, axis=1)


def interact_kernel(slot_ref, arrived_ref, mine_ref, out_ref, vectors_ref, spaced, gram, edge):
    def place(table, carry):
        start = pl.multiple_of(slot_ref[table] * ROWS, ROWS)
        for part in range(4):
            spaced[part, pl.ds(start, ROWS), :] = arrived_ref[part, table].astype(F32)
        return carry

    lax.fori_loop(0, TAB, place, 0, unroll=8)
    bottom = packed_bottom(mine_ref)
    low = jnp.concatenate([low_lanes(TAB)] * 4, axis=1)
    for row in range(ROWS):
        vectors = jnp.concatenate(
            [spaced[part, pl.ds(row, TAB, stride=ROWS), :] for part in range(4)], axis=1
        )
        narrow = vectors.astype(BF16)
        vectors_ref[row] = narrow
        right = jnp.concatenate(
            [jnp.where(low, vectors, 0.0), jnp.where(low, 0.0, vectors)], axis=0
        ).astype(BF16)
        extra = jnp.broadcast_to(bottom[row : row + 1], (ROWS, 512)).astype(BF16)
        product = dot_t(jnp.concatenate([narrow, extra], axis=0), right)
        gram[pl.ds(row, TAB, stride=ROWS), :] = product[0:TAB]
        edge[row : row + 1, :] = product[TAB : TAB + 1]

    lane = lane_iota(ROWS)
    for half in range(2):
        where = slice(half * ROWS, (half + 1) * ROWS)
        out_ref[where, 0:EMB] = mine_ref[where, :].astype(BF16)
        tile, filled = EMB // LANES, jnp.zeros((ROWS, LANES), F32)
        for row, start, count, spot in pieces():
            source = edge[...] if row < 0 else gram[row * ROWS : (row + 1) * ROWS, :]
            moved = turned(source, spot - start - half * HALF)
            for at, first, end in parts_of(spot, count):
                if at != tile:
                    out_ref[where, tile * LANES : (tile + 1) * LANES] = filled.astype(BF16)
                    tile, filled = at, jnp.zeros((ROWS, LANES), F32)
                filled = jnp.where((lane >= first) & (lane < end), moved, filled)
        out_ref[where, tile * LANES : (tile + 1) * LANES] = filled.astype(BF16)


def whole(shape):
    return pl.BlockSpec(shape, lambda *_: (0,) * len(shape))


def interact(table_slot, arrived, mine):
    return pl.pallas_call(
        interact_kernel,
        in_specs=[
            pl.BlockSpec(memory_space=pltpu.SMEM),
            pl.BlockSpec(memory_space=pltpu.VMEM),
            pl.BlockSpec(memory_space=pltpu.VMEM),
        ],
        out_specs=[pl.BlockSpec(memory_space=pltpu.VMEM)] * 2,
        out_shape=[
            jax.ShapeDtypeStruct((2 * ROWS, WIDE), BF16),
            jax.ShapeDtypeStruct((ROWS, TAB, 512), BF16),
        ],
        scratch_shapes=[
            pltpu.VMEM((4, TAB * ROWS, LANES), F32),
            pltpu.VMEM((TAB * ROWS, LANES), F32),
            pltpu.VMEM((ROWS, LANES), F32),
        ],
        compiler_params=pltpu.CompilerParams(vmem_limit_bytes=16 << 20),
        name="interact",
    )(table_slot, arrived, mine)


def top_kernel(f0, f1, f2, f3, weight_ref, out_weight_ref, all_ref, z_ref, partial_ref, delta_ref, hidden_ref):
    for part, ref in enumerate((f0, f1, f2, f3)):
        all_ref[part * 32 : (part + 1) * 32, :] = ref[...]
    weight = weight_ref[...]
    pre = jnp.dot(all_ref[:, 0:FEAT], weight, preferred_element_type=F32)
    sigma = jax.nn.sigmoid(pre)
    hidden = (pre * sigma).astype(BF16)
    slope = sigma * (1.0 + pre * (1.0 - sigma))
    out_weight = out_weight_ref[0:1, :]
    delta = (out_weight * slope).astype(BF16)
    hidden_ref[...] = hidden
    delta_ref[...] = delta
    partial_ref[...] = dot_t(jnp.broadcast_to(out_weight, (16, 512)).astype(BF16), hidden)[0:8]
    z = dot_t(delta, weight).astype(BF16)
    for part in range(4):
        z_ref[part, :, 0:FEAT] = z[part * 32 : (part + 1) * 32]
        z_ref[part, :, FEAT:WIDE] = jnp.zeros((32, WIDE - FEAT), BF16)


def top(parts, top_weight, out_weight):
    return pl.pallas_call(
        top_kernel,
        in_specs=[pl.BlockSpec(memory_space=pltpu.VMEM)] * 6,
        out_specs=[pl.BlockSpec(memory_space=pltpu.VMEM)] * 5,
        out_shape=[
            jax.ShapeDtypeStruct((128, WIDE), BF16),
            jax.ShapeDtypeStruct((4, 32, WIDE), BF16),
            jax.ShapeDtypeStruct((8, LANES), F32),
            jax.ShapeDtypeStruct((128, 512), BF16),
            jax.ShapeDtypeStruct((128, 512), BF16),
        ],
        compiler_params=pltpu.CompilerParams(vmem_limit_bytes=24 << 20),
        name="top",
    )(*parts, top_weight, out_weight)


def weight_grad_kernel(p0, p1, p2, p3, labels_ref, all_ref, delta_ref, hidden_ref, grad_ref, logit_ref, dlogit_ref):
    logits = (p0[...] + turned(p2[...], 64)) + (turned(p1[...], 32) + turned(p3[...], 96))
    logit_ref[...] = logits
    dlogit = (jax.nn.sigmoid(logits) - labels_ref[0:1, :]) * (1.0 / 128.0)
    dlogit_ref[...] = dlogit
    column = dlogit.T[:, 0:1]
    delta = (delta_ref[...].astype(F32) * column).astype(BF16)
    last = WIDE - LANES
    grad_ref[:, 0:last] = lax.dot_general(
        delta, all_ref[:, 0:last], (((0,), (0,)), ((), ())), preferred_element_type=F32
    ).astype(BF16)
    lane = lane_iota(128)
    coarse = column.astype(BF16).astype(F32)
    spots = jnp.where(lane == 32, coarse, jnp.where(lane == 33, column - coarse, 0.0)).astype(BF16)
    grad_ref[:, last:WIDE] = lax.dot_general(
        jnp.concatenate([delta, hidden_ref[...]], axis=0),
        jnp.concatenate([all_ref[:, last:WIDE], spots], axis=0),
        (((0,), (0,)), ((), ())),
        preferred_element_type=F32,
    ).astype(BF16)


def weight_grad(partials, labels, features, delta, hidden):
    return pl.pallas_call(
        weight_grad_kernel,
        in_specs=[pl.BlockSpec(memory_space=pltpu.VMEM)] * 8,
        out_specs=[pl.BlockSpec(memory_space=pltpu.VMEM)] * 3,
        out_shape=[
            jax.ShapeDtypeStruct((512, WIDE), BF16),
            jax.ShapeDtypeStruct((8, LANES), F32),
            jax.ShapeDtypeStruct((8, LANES), F32),
        ],
        compiler_params=pltpu.CompilerParams(vmem_limit_bytes=24 << 20),
        name="weight_grad",
    )(*partials, labels, features, delta, hidden)


def spread_kernel(
    slot_ref, z0, z1, z2, z3, dlogit_ref, vectors_ref, mine_ref, slope_ref, dense_ref,
    back_ref, bottom_ref, dfeat, upper, edge, right, dvec, dedge,
):
    column = dlogit_ref[...].T[0:32, 0:1]
    summed = z0[...].astype(F32) + z1[...].astype(F32) + z2[...].astype(F32) + z3[...].astype(F32)
    dfeat[...] = summed * column
    lane = lane_iota(ROWS)
    for row, start, count, spot in pieces():
        filled = jnp.zeros((ROWS, LANES), F32)
        for half in range(2):
            for at, first, end in parts_of(spot, count):
                source = dfeat[half * ROWS : (half + 1) * ROWS, at * LANES : (at + 1) * LANES]
                moved = turned(source, start + half * HALF - spot)
                shift = start + half * HALF - spot + at * LANES
                inside = (lane >= first + shift) & (lane < end + shift)
                filled = jnp.where(inside, moved, filled)
        filled = filled.astype(BF16).astype(F32)
        if row < 0:
            edge[...] = filled
        else:
            upper[row * ROWS : (row + 1) * ROWS, :] = filled
    upper[(TAB - 1) * ROWS :, :] = jnp.zeros((ROWS, LANES), F32)
    right[...] = jnp.zeros_like(right)
    bottom = packed_bottom(mine_ref)
    low = low_lanes(TAB)
    low_wide = jnp.concatenate([low] * 4, axis=1)
    low_few = jnp.concatenate([low_lanes(16)] * 4, axis=1)
    top_row = lax.broadcasted_iota(jnp.int32, (16, 512), 0) == 0
    for row in range(ROWS):
        half = upper[pl.ds(row, TAB, stride=ROWS), :]
        zeroth = jnp.broadcast_to(edge[row : row + 1, :], (TAB, LANES))
        flipped = jnp.concatenate([half, zeroth], axis=0).T
        first, second = flipped[0:TAB], turned(flipped[TAB : 2 * TAB], HALF)
        whole_matrix = half + jnp.where(low, first, second)
        edges = jnp.where(low, second, first)
        left = jnp.concatenate(
            [
                jnp.concatenate([whole_matrix, edges], axis=1),
                jnp.concatenate([zeroth[0:16], jnp.zeros((16, LANES), F32)], axis=1),
            ],
            axis=0,
        ).astype(BF16)
        vectors = vectors_ref[row].astype(F32)
        right[0:TAB, :] = jnp.where(low_wide, vectors, 0.0).astype(BF16)
        right[TAB : 2 * TAB, :] = jnp.where(low_wide, 0.0, vectors).astype(BF16)
        own = jnp.broadcast_to(bottom[row : row + 1], (16, 512))
        right[128:144, :] = jnp.where(top_row & ~low_few, own, 0.0).astype(BF16)
        right[192:208, :] = jnp.where(top_row & low_few, own, 0.0).astype(BF16)
        product = jnp.dot(left, right[...], preferred_element_type=F32)
        for part in range(4):
            lanes = slice(part * LANES, (part + 1) * LANES)
            dvec[part, pl.ds(row, TAB, stride=ROWS), :] = product[0:TAB, lanes]
        dedge[row : row + 1, :] = product[TAB : TAB + 1]

    def place(table, carry):
        start = pl.multiple_of(slot_ref[table] * ROWS, ROWS)
        for part in range(4):
            back_ref[part, table] = dvec[part, pl.ds(start, ROWS), :].astype(BF16)
        return carry

    lax.fori_loop(0, TAB, place, 0, unroll=8)
    low = low_lanes(ROWS)
    tiles = [dedge[:, part * LANES : (part + 1) * LANES] for part in range(4)]
    own_rows = [
        jnp.concatenate(
            [jnp.where(low, tiles[2 * p], turned(tiles[2 * p + 1], HALF)) for p in range(2)], axis=1
        ),
        jnp.concatenate(
            [jnp.where(low, turned(tiles[2 * p], HALF), tiles[2 * p + 1]) for p in range(2)], axis=1
        ),
    ]
    dbottom = (dfeat[:, 0:EMB] + jnp.concatenate(own_rows, axis=0)) * slope_ref[...]
    bottom_ref[...] = lax.dot_general(
        dense_ref[...],
        dbottom,
        (((0,), (0,)), ((), ())),
        precision=lax.Precision.HIGHEST,
        preferred_element_type=F32,
    )


def spread(table_slot, zs, dlogit, vectors, mine, slope, dense):
    return pl.pallas_call(
        spread_kernel,
        in_specs=[pl.BlockSpec(memory_space=pltpu.SMEM)]
        + [pl.BlockSpec(memory_space=pltpu.VMEM)] * 9,
        out_specs=[pl.BlockSpec(memory_space=pltpu.VMEM)] * 2,
        out_shape=[
            jax.ShapeDtypeStruct((4, TAB, ROWS, LANES), BF16),
            jax.ShapeDtypeStruct((16, EMB), F32),
        ],
        scratch_shapes=[
            pltpu.VMEM((2 * ROWS, WIDE), F32),
            pltpu.VMEM((TAB * ROWS, LANES), F32),
            pltpu.VMEM((ROWS, LANES), F32),
            pltpu.VMEM((256, 512), BF16),
            pltpu.VMEM((4, TAB * ROWS, LANES), F32),
            pltpu.VMEM((ROWS, 512), F32),
        ],
        compiler_params=pltpu.CompilerParams(vmem_limit_bytes=16 << 20),
        name="spread",
    )(table_slot, *zs, dlogit, vectors, mine, slope, dense)


def row_grad_kernel(index_ref, length_ref, back_ref, out_ref, total, counted, moved):
    step = pl.program_id(0)

    @pl.when(step == 0)
    def _():
        total[...] = jnp.zeros_like(total)

    values = lax.broadcasted_iota(jnp.int32, (256, LANES), 0)
    low = low_lanes(HALF)
    for group in range(STEP):
        lanes = slice(group * LANES, (group + 1) * LANES)
        length = length_ref[0:1, lanes]
        counts = jnp.zeros((256, LANES), F32)
        for slot in range(4):
            ids = jnp.where(slot < length, index_ref[0, slot : slot + 1, lanes], -1)
            counts = counts + jnp.where(ids == values, 1.0, 0.0)
        counted[:, lanes] = counts.astype(BF16)
        rows = jnp.concatenate([back_ref[peer, group].astype(F32) for peer in range(4)], axis=0)
        moved[group * LANES : group * LANES + HALF, :] = jnp.where(low, rows, 0.0).astype(BF16)
        moved[group * LANES + HALF : (group + 1) * LANES, :] = jnp.where(low, 0.0, rows).astype(BF16)
    total[...] += jnp.dot(counted[...], moved[...], preferred_element_type=F32)

    @pl.when(step == pl.num_programs(0) - 1)
    def _():
        flipped = total[...].T
        out_ref[0] = flipped[0:HALF] + flipped[HALF:LANES]


def row_grad(pool_index, bag_length, back):
    return pl.pallas_call(
        row_grad_kernel,
        grid=(TAB // STEP,),
        in_specs=[
            pl.BlockSpec((1, 4, STEP * LANES), lambda i: (0, 0, i)),
            pl.BlockSpec((1, STEP * LANES), lambda i: (0, i)),
            pl.BlockSpec((4, STEP, ROWS, LANES), lambda i: (0, i, 0, 0)),
        ],
        out_specs=pl.BlockSpec((1, HALF, 256), lambda i: (0, 0, 0)),
        out_shape=jax.ShapeDtypeStruct((1, HALF, 256), F32),
        scratch_shapes=[
            pltpu.VMEM((256, LANES), F32),
            pltpu.VMEM((256, STEP * LANES), BF16),
            pltpu.VMEM((STEP * LANES, LANES), BF16),
        ],
        compiler_params=pltpu.CompilerParams(vmem_limit_bytes=12 << 20),
        name="row_grad",
    )(pool_index, bag_length, back)


def shifted(x, axis, shift):
    size = lax.axis_size(axis)
    return lax.ppermute(x, axis, [(i, (i + shift) % size) for i in range(size)])


def exchange(x, axes):
    return lax.all_to_all(x, axes, split_axis=0, concat_axis=0, tiled=True)


def summed_over(x, axis):
    if lax.axis_size(axis) == 2:
        return x + shifted(x, axis, 1)
    return (x + shifted(x, axis, 2)) + (shifted(x, axis, 1) + shifted(x, axis, 3))


def silu_slope(values):
    sigma = jax.nn.sigmoid(values)
    return sigma * (1.0 + values * (1.0 - sigma))


def picked(x, which):
    return lax.dynamic_index_in_dim(x, which, 1, keepdims=False)


def body(
    table_rows,
    pool_index,
    bag_length,
    table_slot,
    dense_input,
    bottom_weight,
    top_weight,
    out_weight,
    labels,
):
    me = lax.axis_index("col")
    rows = jnp.transpose(table_rows, (0, 2, 1))
    pooled = pool(pool_index, bag_length, rows)
    arrived = exchange(pooled.reshape(4 * TAB, ROWS, LANES), COL_GRP).reshape(4, TAB, ROWS, LANES)

    dense_mine = lax.dynamic_index_in_dim(
        dense_input.reshape(2, 4, ROWS, -1), me, 1, keepdims=False
    ).reshape(2 * ROWS, -1)
    mine_pre = jnp.dot(dense_mine, bottom_weight, preferred_element_type=F32)
    mine = jax.nn.silu(mine_pre).astype(BF16).astype(F32)
    mine_slope = silu_slope(mine_pre)
    dense_wide = jnp.pad(dense_mine.astype(F32), ((0, 0), (0, 16 - dense_mine.shape[1])))
    order = (me - jnp.arange(4)) % 4
    labels_rel = jnp.take(
        jnp.transpose(labels.reshape(2, 4, ROWS), (1, 0, 2)), order, axis=0
    ).reshape(1, LANES).astype(F32)
    out_weight_row = out_weight.astype(F32).reshape(1, -1)

    part, vectors = interact(table_slot, arrived, mine)
    parts = [part] + [shifted(part, "col", away) for away in (1, 2, 3)]
    features, z, partial, delta, hidden = top(parts, top_weight, out_weight_row)
    partials = [partial] + [shifted(partial, "col", away) for away in (1, 2, 3)]
    zs = [z[0]] + [shifted(z[away], "col", -away) for away in (1, 2, 3)]
    grad, logits_rel, dlogit = weight_grad(partials, labels_rel, features, delta, hidden)
    back, bottom_part = spread(table_slot, zs, dlogit, vectors, mine, mine_slope, dense_wide)
    returned = exchange(back.reshape(4 * TAB, ROWS, LANES), COL_GRP).reshape(4, TAB, ROWS, LANES)
    grad_rows = jnp.transpose(row_grad(pool_index, bag_length, returned), (0, 2, 1))

    logits = jnp.take(logits_rel[0].reshape(4, 2, ROWS), order, axis=0)
    logits = jnp.transpose(logits, (1, 0, 2)).reshape(LANES)

    core, upper = lax.axis_index("grp_3"), lax.axis_index("grp_1")
    grad = grad.reshape(32, 2, 8, WIDE)
    other = shifted(picked(grad, 1 - core), "grp_3", 1)
    grad = picked(grad, core).astype(F32) + other.astype(F32)
    grad = jnp.transpose(grad.astype(BF16).reshape(4, 2, 4, 8, WIDE), (0, 2, 1, 3, 4))
    grad = exchange(grad.reshape(16, 16, WIDE), ("grp_0", "grp_2"))
    grad = jnp.sum(grad.astype(F32), axis=0).reshape(1, 2, 8, WIDE)
    other = shifted(picked(grad, 1 - upper).astype(BF16), "grp_1", 1)
    grad = (picked(grad, upper) + other.astype(F32))[0]
    grad_top = jnp.transpose(grad[:, 0:FEAT])
    grad_out = grad[:, FEAT] + grad[:, FEAT + 1]

    bottom = bottom_part
    for axis in ("grp_3", "col", "grp_0", "grp_2", "grp_1"):
        bottom = summed_over(bottom, axis)
    grad_bottom = bottom[0 : bottom_weight.shape[0]]
    return (logits, grad_top, grad_out, grad_bottom, grad_rows)


def solution(mesh):
    torus = Mesh(
        mesh.devices.reshape(mesh.shape["col"], 4, 2, 4, 2),
        ("col", "grp_0", "grp_1", "grp_2", "grp_3"),
    )
    return jax.shard_map(
        body,
        mesh=torus,
        in_specs=(
            P(GRP, None, "col"),
            P(GRP, None, None),
            P(GRP, None),
            P(),
            P(GRP, None),
            P(),
            P(None, "col"),
            P("col"),
            P(GRP),
        ),
        out_specs=(P(GRP), P(None, COL_GRP), P(COL_GRP), P(), P(GRP, None, "col")),
        check_vma=False,
    )
```

```python
import jax
import jax.numpy as jnp
from jax import lax
from jax.experimental import pallas as pl
from jax.experimental.pallas import tpu as pltpu
from jax.sharding import Mesh
from jax.sharding import PartitionSpec as P


COL_GRP = ("col", "grp_0", "grp_1", "grp_2", "grp_3")
GRP = ("grp_0", "grp_1", "grp_2", "grp_3")
F32 = jnp.float32
BF16 = jnp.bfloat16

TAB = 64
ROWS = 16
LANES = 128
HALF = 64
EMB = 256
FEAT = 2336
WIDE = 2432
STEP = 8


def pieces():
    found = [(-1, 0, TAB, EMB)]
    place = EMB + TAB
    for row in range(TAB - 1):
        found.append((row, row + 1, TAB - 1 - row, place))
        place += TAB - 1 - row
    return found


def parts_of(place, count):
    found = []
    for tile in range(place // LANES, (place + count - 1) // LANES + 1):
        first = max(place, tile * LANES) - tile * LANES
        end = min(place + count, (tile + 1) * LANES) - tile * LANES
        found.append((tile, first, end))
    return found


def lane_iota(rows):
    return lax.broadcasted_iota(jnp.int32, (rows, LANES), 1)


def low_lanes(rows):
    return lane_iota(rows) < HALF


def turned(x, shift):
    shift %= LANES
    return x if shift == 0 else pltpu.roll(x, shift, 1)


def dot_t(a, b):
    return lax.dot_general(a, b, (((1,), (1,)), ((), ())), preferred_element_type=F32)


def hbm(shape, dtype):
    return pltpu.HBM(shape, dtype)


def vmem_specs(count):
    return [pl.BlockSpec(memory_space=pltpu.VMEM)] * count


def pool_kernel(index_ref, length_ref, rows_ref, out_ref, weights, counted):
    @pl.when(pl.program_id(0) == 0)
    def _():
        weights[...] = jnp.zeros_like(weights)
        weights[0:HALF, 0:256] = rows_ref[0]
        weights[HALF:LANES, 256:512] = rows_ref[0]

    values = lax.broadcasted_iota(jnp.int32, (LANES, 256), 1)
    slots = lax.broadcasted_iota(jnp.int32, (8, LANES), 0)
    for group in range(STEP):
        lanes = slice(group * LANES, (group + 1) * LANES)
        index = index_ref[0, :, lanes]
        index = jnp.concatenate([index, index], axis=0)
        ids = jnp.where(slots < length_ref[0:1, lanes], index, -1).T
        counts = jnp.zeros((LANES, 256), F32)
        for slot in range(4):
            counts = counts + jnp.where(ids[:, slot : slot + 1] == values, 1.0, 0.0)
        counts = counts.astype(BF16)
        counted[group * HALF : (group + 1) * HALF, 0:256] = counts[0:HALF]
        counted[group * HALF : (group + 1) * HALF, 256:512] = counts[HALF:LANES]
    pooled = dot_t(counted[...], weights[...]).astype(BF16)
    for group in range(STEP):
        for peer in range(4):
            first = group * HALF + peer * ROWS
            out_ref[peer, group] = pooled[first : first + ROWS]


def pool(pool_index, bag_length, rows):
    return pl.pallas_call(
        pool_kernel,
        grid=(TAB // STEP,),
        in_specs=[
            pl.BlockSpec((1, 4, STEP * LANES), lambda i: (0, 0, i)),
            pl.BlockSpec((1, STEP * LANES), lambda i: (0, i)),
            pl.BlockSpec((1, HALF, 256), lambda i: (0, 0, 0)),
        ],
        out_specs=pl.BlockSpec((4, STEP, ROWS, LANES), lambda i: (0, i, 0, 0)),
        out_shape=hbm((4, TAB, ROWS, LANES), BF16),
        scratch_shapes=[
            pltpu.VMEM((LANES, 512), BF16),
            pltpu.VMEM((STEP * HALF, 512), BF16),
        ],
        compiler_params=pltpu.CompilerParams(vmem_limit_bytes=12 << 20),
        name="pool",
    )(pool_index, bag_length, rows)


def packed_bottom(mine_ref):
    low = low_lanes(ROWS)
    tiles = []
    for pair in range(2):
        lanes = slice(pair * LANES, (pair + 1) * LANES)
        first, second = mine_ref[0:ROWS, lanes], mine_ref[ROWS : 2 * ROWS, lanes]
        tiles.append(jnp.where(low, first, turned(second, HALF)))
        tiles.append(jnp.where(low, turned(first, HALF), second))
    return jnp.concatenate(tiles, axis=1)


def interact_kernel(slot_ref, arrived_ref, mine_ref, out_ref, vectors_ref, spaced, gram, edge):
    def place(table, carry):
        start = pl.multiple_of(slot_ref[table] * ROWS, ROWS)
        for part in range(4):
            spaced[part, pl.ds(start, ROWS), :] = arrived_ref[part, table].astype(F32)
        return carry

    lax.fori_loop(0, TAB, place, 0, unroll=8)
    bottom = packed_bottom(mine_ref)
    low = jnp.concatenate([low_lanes(TAB)] * 4, axis=1)
    for row in range(ROWS):
        vectors = jnp.concatenate(
            [spaced[part, pl.ds(row, TAB, stride=ROWS), :] for part in range(4)], axis=1
        )
        narrow = vectors.astype(BF16)
        vectors_ref[row] = narrow
        right = jnp.concatenate(
            [jnp.where(low, vectors, 0.0), jnp.where(low, 0.0, vectors)], axis=0
        ).astype(BF16)
        extra = jnp.broadcast_to(bottom[row : row + 1], (ROWS, 512)).astype(BF16)
        product = dot_t(jnp.concatenate([narrow, extra], axis=0), right)
        gram[pl.ds(row, TAB, stride=ROWS), :] = product[0:TAB]
        edge[row : row + 1, :] = product[TAB : TAB + 1]

    lane = lane_iota(ROWS)
    for half in range(2):
        where = slice(half * ROWS, (half + 1) * ROWS)
        out_ref[where, 0:EMB] = mine_ref[where, :].astype(BF16)
        tile, filled = EMB // LANES, jnp.zeros((ROWS, LANES), F32)
        for row, start, count, spot in pieces():
            source = edge[...] if row < 0 else gram[row * ROWS : (row + 1) * ROWS, :]
            moved = turned(source, spot - start - half * HALF)
            for at, first, end in parts_of(spot, count):
                if at != tile:
                    out_ref[where, tile * LANES : (tile + 1) * LANES] = filled.astype(BF16)
                    tile, filled = at, jnp.zeros((ROWS, LANES), F32)
                filled = jnp.where((lane >= first) & (lane < end), moved, filled)
        out_ref[where, tile * LANES : (tile + 1) * LANES] = filled.astype(BF16)


def interact(table_slot, arrived, mine):
    return pl.pallas_call(
        interact_kernel,
        in_specs=[
            pl.BlockSpec(memory_space=pltpu.SMEM),
            pl.BlockSpec(memory_space=pltpu.VMEM),
            pl.BlockSpec(memory_space=pltpu.VMEM),
        ],
        out_specs=[pl.BlockSpec(memory_space=pltpu.VMEM)] * 2,
        out_shape=[
            jax.ShapeDtypeStruct((2 * ROWS, WIDE), BF16),
            hbm((ROWS, TAB, 512), BF16),
        ],
        scratch_shapes=[
            pltpu.VMEM((4, TAB * ROWS, LANES), F32),
            pltpu.VMEM((TAB * ROWS, LANES), F32),
            pltpu.VMEM((ROWS, LANES), F32),
        ],
        compiler_params=pltpu.CompilerParams(vmem_limit_bytes=16 << 20),
        name="interact",
    )(table_slot, arrived, mine)


def top_kernel(
    f0, f1, f2, f3, weight_ref, out_weight_ref,
    all_ref, z0, z1, z2, z3, partial_ref, delta_ref, hidden_ref,
):
    for part, ref in enumerate((f0, f1, f2, f3)):
        all_ref[part * 32 : (part + 1) * 32, :] = ref[...]
    weight = weight_ref[...]
    pre = jnp.dot(all_ref[:, 0:FEAT], weight, preferred_element_type=F32)
    sigma = jax.nn.sigmoid(pre)
    hidden = (pre * sigma).astype(BF16)
    slope = sigma * (1.0 + pre * (1.0 - sigma))
    out_weight = out_weight_ref[0:1, :]
    delta = (out_weight * slope).astype(BF16)
    hidden_ref[...] = hidden
    delta_ref[...] = delta
    partial_ref[...] = dot_t(jnp.broadcast_to(out_weight, (16, 512)).astype(BF16), hidden)[0:8]
    z = dot_t(delta, weight).astype(BF16)
    for part, ref in enumerate((z0, z1, z2, z3)):
        ref[:, 0:FEAT] = z[part * 32 : (part + 1) * 32]
        ref[:, FEAT:WIDE] = jnp.zeros((32, WIDE - FEAT), BF16)


def top(parts, top_weight, out_weight):
    return pl.pallas_call(
        top_kernel,
        in_specs=vmem_specs(6),
        out_specs=vmem_specs(8),
        out_shape=[hbm((128, WIDE), BF16), hbm((32, WIDE), BF16)]
        + [jax.ShapeDtypeStruct((32, WIDE), BF16)] * 3
        + [
            jax.ShapeDtypeStruct((8, LANES), F32),
            hbm((128, 512), BF16),
            hbm((128, 512), BF16),
        ],
        compiler_params=pltpu.CompilerParams(vmem_limit_bytes=24 << 20),
        name="top",
    )(*parts, top_weight, out_weight)


def weight_grad_kernel(
    core_ref, p0, p1, p2, p3, labels_ref, all_ref, delta_ref, hidden_ref,
    own_ref, other_ref, logit_ref, dlogit_ref, grad,
):
    logits = (p0[...] + turned(p2[...], 64)) + (turned(p1[...], 32) + turned(p3[...], 96))
    logit_ref[...] = logits
    dlogit = (jax.nn.sigmoid(logits) - labels_ref[0:1, :]) * (1.0 / 128.0)
    dlogit_ref[...] = dlogit
    column = dlogit.T[:, 0:1]
    delta = (delta_ref[...].astype(F32) * column).astype(BF16)
    last = WIDE - LANES
    grad[:, 0:last] = lax.dot_general(
        delta, all_ref[:, 0:last], (((0,), (0,)), ((), ())), preferred_element_type=F32
    )
    lane = lane_iota(128)
    coarse = column.astype(BF16).astype(F32)
    spots = jnp.where(lane == 32, coarse, jnp.where(lane == 33, column - coarse, 0.0)).astype(BF16)
    grad[:, last:WIDE] = lax.dot_general(
        jnp.concatenate([delta, hidden_ref[...]], axis=0),
        jnp.concatenate([all_ref[:, last:WIDE], spots], axis=0),
        (((0,), (0,)), ((), ())),
        preferred_element_type=F32,
    )
    core = core_ref[0]
    for x in range(4):
        for y in range(4):
            for ref, which in ((own_ref, core), (other_ref, 1 - core)):
                both = []
                for z in range(2):
                    first = pl.multiple_of((((x * 2 + z) * 4 + y) * 2 + which) * 8, 8)
                    both.append(grad[pl.ds(first, 8), :])
                ref[x * 4 + y] = jnp.concatenate(both, axis=0).astype(BF16)


def weight_grad(core, partials, labels, features, delta, hidden):
    return pl.pallas_call(
        weight_grad_kernel,
        in_specs=[pl.BlockSpec(memory_space=pltpu.SMEM)] + vmem_specs(8),
        out_specs=vmem_specs(4),
        out_shape=[
            hbm((16, 16, WIDE), BF16),
            hbm((16, 16, WIDE), BF16),
            jax.ShapeDtypeStruct((8, LANES), F32),
            jax.ShapeDtypeStruct((8, LANES), F32),
        ],
        scratch_shapes=[pltpu.VMEM((512, WIDE), F32)],
        compiler_params=pltpu.CompilerParams(vmem_limit_bytes=32 << 20),
        name="weight_grad",
    )(core, *partials, labels, features, delta, hidden)


def spread_kernel(
    slot_ref, z0, z1, z2, z3, dlogit_ref, vectors_ref, mine_ref, slope_ref, dense_ref,
    back_ref, bottom_ref, dfeat, upper, edge, right, dvec, dedge,
):
    column = dlogit_ref[...].T[0:32, 0:1]
    summed = z0[...].astype(F32) + z1[...].astype(F32) + z2[...].astype(F32) + z3[...].astype(F32)
    dfeat[...] = summed * column
    lane = lane_iota(ROWS)
    for row, start, count, spot in pieces():
        filled = jnp.zeros((ROWS, LANES), F32)
        for half in range(2):
            for at, first, end in parts_of(spot, count):
                source = dfeat[half * ROWS : (half + 1) * ROWS, at * LANES : (at + 1) * LANES]
                moved = turned(source, start + half * HALF - spot)
                shift = start + half * HALF - spot + at * LANES
                inside = (lane >= first + shift) & (lane < end + shift)
                filled = jnp.where(inside, moved, filled)
        filled = filled.astype(BF16).astype(F32)
        if row < 0:
            edge[...] = filled
        else:
            upper[row * ROWS : (row + 1) * ROWS, :] = filled
    upper[(TAB - 1) * ROWS :, :] = jnp.zeros((ROWS, LANES), F32)
    right[...] = jnp.zeros_like(right)
    bottom = packed_bottom(mine_ref)
    low = low_lanes(TAB)
    low_wide = jnp.concatenate([low] * 4, axis=1)
    low_few = jnp.concatenate([low_lanes(16)] * 4, axis=1)
    top_row = lax.broadcasted_iota(jnp.int32, (16, 512), 0) == 0
    for row in range(ROWS):
        half = upper[pl.ds(row, TAB, stride=ROWS), :]
        zeroth = jnp.broadcast_to(edge[row : row + 1, :], (TAB, LANES))
        flipped = jnp.concatenate([half, zeroth], axis=0).T
        first, second = flipped[0:TAB], turned(flipped[TAB : 2 * TAB], HALF)
        whole_matrix = half + jnp.where(low, first, second)
        edges = jnp.where(low, second, first)
        left = jnp.concatenate(
            [
                jnp.concatenate([whole_matrix, edges], axis=1),
                jnp.concatenate([zeroth[0:16], jnp.zeros((16, LANES), F32)], axis=1),
            ],
            axis=0,
        ).astype(BF16)
        vectors = vectors_ref[row].astype(F32)
        right[0:TAB, :] = jnp.where(low_wide, vectors, 0.0).astype(BF16)
        right[TAB : 2 * TAB, :] = jnp.where(low_wide, 0.0, vectors).astype(BF16)
        own = jnp.broadcast_to(bottom[row : row + 1], (16, 512))
        right[128:144, :] = jnp.where(top_row & ~low_few, own, 0.0).astype(BF16)
        right[192:208, :] = jnp.where(top_row & low_few, own, 0.0).astype(BF16)
        product = jnp.dot(left, right[...], preferred_element_type=F32)
        for part in range(4):
            lanes = slice(part * LANES, (part + 1) * LANES)
            dvec[part, pl.ds(row, TAB, stride=ROWS), :] = product[0:TAB, lanes]
        dedge[row : row + 1, :] = product[TAB : TAB + 1]

    def place(table, carry):
        start = pl.multiple_of(slot_ref[table] * ROWS, ROWS)
        for part in range(4):
            back_ref[part, table] = dvec[part, pl.ds(start, ROWS), :].astype(BF16)
        return carry

    lax.fori_loop(0, TAB, place, 0, unroll=8)
    low = low_lanes(ROWS)
    tiles = [dedge[:, part * LANES : (part + 1) * LANES] for part in range(4)]
    own_rows = [
        jnp.concatenate(
            [jnp.where(low, tiles[2 * p], turned(tiles[2 * p + 1], HALF)) for p in range(2)], axis=1
        ),
        jnp.concatenate(
            [jnp.where(low, turned(tiles[2 * p], HALF), tiles[2 * p + 1]) for p in range(2)], axis=1
        ),
    ]
    dbottom = (dfeat[:, 0:EMB] + jnp.concatenate(own_rows, axis=0)) * slope_ref[...]
    bottom_ref[...] = lax.dot_general(
        dense_ref[...],
        dbottom,
        (((0,), (0,)), ((), ())),
        precision=lax.Precision.HIGHEST,
        preferred_element_type=F32,
    )


def spread(table_slot, zs, dlogit, vectors, mine, slope, dense):
    return pl.pallas_call(
        spread_kernel,
        in_specs=[pl.BlockSpec(memory_space=pltpu.SMEM)]
        + [pl.BlockSpec(memory_space=pltpu.VMEM)] * 9,
        out_specs=[pl.BlockSpec(memory_space=pltpu.VMEM)] * 2,
        out_shape=[
            hbm((4, TAB, ROWS, LANES), BF16),
            jax.ShapeDtypeStruct((16, EMB), F32),
        ],
        scratch_shapes=[
            pltpu.VMEM((2 * ROWS, WIDE), F32),
            pltpu.VMEM((TAB * ROWS, LANES), F32),
            pltpu.VMEM((ROWS, LANES), F32),
            pltpu.VMEM((256, 512), BF16),
            pltpu.VMEM((4, TAB * ROWS, LANES), F32),
            pltpu.VMEM((ROWS, 512), F32),
        ],
        compiler_params=pltpu.CompilerParams(vmem_limit_bytes=16 << 20),
        name="spread",
    )(table_slot, *zs, dlogit, vectors, mine, slope, dense)


def row_grad_kernel(index_ref, length_ref, back_ref, out_ref, total, counted, moved):
    step = pl.program_id(0)

    @pl.when(step == 0)
    def _():
        total[...] = jnp.zeros_like(total)

    values = lax.broadcasted_iota(jnp.int32, (256, LANES), 0)
    low = low_lanes(HALF)
    for group in range(STEP):
        lanes = slice(group * LANES, (group + 1) * LANES)
        length = length_ref[0:1, lanes]
        counts = jnp.zeros((256, LANES), F32)
        for slot in range(4):
            ids = jnp.where(slot < length, index_ref[0, slot : slot + 1, lanes], -1)
            counts = counts + jnp.where(ids == values, 1.0, 0.0)
        counted[:, lanes] = counts.astype(BF16)
        rows = jnp.concatenate([back_ref[peer, group].astype(F32) for peer in range(4)], axis=0)
        moved[group * LANES : group * LANES + HALF, :] = jnp.where(low, rows, 0.0).astype(BF16)
        moved[group * LANES + HALF : (group + 1) * LANES, :] = jnp.where(low, 0.0, rows).astype(BF16)
    total[...] += jnp.dot(counted[...], moved[...], preferred_element_type=F32)

    @pl.when(step == pl.num_programs(0) - 1)
    def _():
        flipped = total[...].T
        out_ref[0] = flipped[0:HALF] + flipped[HALF:LANES]


def row_grad(pool_index, bag_length, back):
    return pl.pallas_call(
        row_grad_kernel,
        grid=(TAB // STEP,),
        in_specs=[
            pl.BlockSpec((1, 4, STEP * LANES), lambda i: (0, 0, i)),
            pl.BlockSpec((1, STEP * LANES), lambda i: (0, i)),
            pl.BlockSpec((4, STEP, ROWS, LANES), lambda i: (0, i, 0, 0)),
        ],
        out_specs=pl.BlockSpec((1, HALF, 256), lambda i: (0, 0, 0)),
        out_shape=jax.ShapeDtypeStruct((1, HALF, 256), F32),
        scratch_shapes=[
            pltpu.VMEM((256, LANES), F32),
            pltpu.VMEM((256, STEP * LANES), BF16),
            pltpu.VMEM((STEP * LANES, LANES), BF16),
        ],
        compiler_params=pltpu.CompilerParams(vmem_limit_bytes=12 << 20),
        name="row_grad",
    )(pool_index, bag_length, back)


def shifted(x, axis, shift):
    size = lax.axis_size(axis)
    return lax.ppermute(x, axis, [(i, (i + shift) % size) for i in range(size)])


def exchange_all(x):
    flat = x.reshape(4 * TAB, ROWS, LANES)
    flat = lax.all_to_all(flat, COL_GRP, split_axis=0, concat_axis=0, tiled=True)
    return flat.reshape(4, TAB, ROWS, LANES)


def summed_over(x, axis):
    if lax.axis_size(axis) == 2:
        return x + shifted(x, axis, 1)
    others = [shifted(x, axis, shift) for shift in (1, 2, 3)]
    return (x + others[1]) + (others[0] + others[2])


def reduced_to(x, axis):
    me = lax.axis_index(axis)
    size = lax.axis_size(axis)
    total = lax.dynamic_index_in_dim(x, me, 0, keepdims=False).astype(F32)
    for shift in range(1, size):
        block = lax.dynamic_index_in_dim(x, (me + shift) % size, 0, keepdims=False)
        total = total + shifted(block.astype(BF16), axis, shift).astype(F32)
    return total


def silu_slope(values):
    sigma = jax.nn.sigmoid(values)
    return sigma * (1.0 + values * (1.0 - sigma))


def step(
    table_rows,
    pool_index,
    bag_length,
    table_slot,
    dense_input,
    bottom_weight,
    top_weight,
    out_weight,
    labels,
):
    me, core = lax.axis_index("col"), lax.axis_index("grp_3")
    rows = jnp.transpose(table_rows, (0, 2, 1))
    pooled = pool(pool_index, bag_length, rows)
    arrived = exchange_all(pooled)

    dense_mine = lax.dynamic_index_in_dim(
        dense_input.reshape(2, 4, ROWS, -1), me, 1, keepdims=False
    ).reshape(2 * ROWS, -1)
    mine_pre = jnp.dot(dense_mine, bottom_weight, preferred_element_type=F32)
    mine = jax.nn.silu(mine_pre).astype(BF16).astype(F32)
    mine_slope = silu_slope(mine_pre)
    dense_wide = jnp.pad(dense_mine.astype(F32), ((0, 0), (0, 16 - dense_mine.shape[1])))
    order = (me - jnp.arange(4)) % 4
    labels_rel = jnp.take(
        jnp.transpose(labels.reshape(2, 4, ROWS), (1, 0, 2)), order, axis=0
    ).reshape(1, LANES).astype(F32)
    out_weight_row = out_weight.astype(F32).reshape(1, -1)

    part, vectors = interact(table_slot, arrived, mine)
    parts = [part] + [shifted(part, "col", away) for away in (1, 2, 3)]
    features, *zs, partial, delta, hidden = top(parts, top_weight, out_weight_row)
    zs = [zs[0]] + [shifted(zs[away], "col", -away) for away in (1, 2, 3)]
    partials = [partial] + [shifted(partial, "col", away) for away in (1, 2, 3)]
    own, other, logits_rel, dlogit = weight_grad(
        core.astype(jnp.int32).reshape(1), partials, labels_rel, features, delta, hidden
    )
    back, bottom = spread(table_slot, zs, dlogit, vectors, mine, mine_slope, dense_wide)
    returned = exchange_all(back)
    grad_rows = jnp.transpose(row_grad(pool_index, bag_length, returned), (0, 2, 1))

    logits = jnp.take(logits_rel[0].reshape(4, 2, ROWS), order, axis=0)
    logits = jnp.transpose(logits, (1, 0, 2)).reshape(LANES)

    other = shifted(other, "grp_3", 1)
    grad = (own.astype(F32) + other.astype(F32)).astype(BF16).reshape(4, 64, WIDE)
    grad = reduced_to(grad, "grp_0").reshape(4, 16, WIDE)
    grad = reduced_to(grad, "grp_2").reshape(2, 8, WIDE)
    grad = reduced_to(grad, "grp_1")
    grad_top = jnp.transpose(grad[:, 0:FEAT])
    grad_out = grad[:, FEAT] + grad[:, FEAT + 1]

    for axis in ("grp_3", "grp_0", "grp_2", "col", "grp_1"):
        bottom = summed_over(bottom, axis)
    grad_bottom = bottom[0 : bottom_weight.shape[0]]
    return (logits, grad_top, grad_out, grad_bottom, grad_rows)


def solution(mesh):
    torus = Mesh(
        mesh.devices.reshape(mesh.shape["col"], 4, 2, 4, 2),
        ("col", "grp_0", "grp_1", "grp_2", "grp_3"),
    )
    return jax.shard_map(
        step,
        mesh=torus,
        in_specs=(
            P(GRP, None, "col"),
            P(GRP, None, None),
            P(GRP, None),
            P(),
            P(GRP, None),
            P(),
            P(None, "col"),
            P("col"),
            P(GRP),
        ),
        out_specs=(P(GRP), P(None, COL_GRP), P(COL_GRP), P(), P(GRP, None, "col")),
        check_vma=False,
    )
```

```python
import jax
import jax.numpy as jnp
from jax import lax
from jax.experimental import pallas as pl
from jax.experimental.pallas import tpu as pltpu
from jax.sharding import Mesh
from jax.sharding import PartitionSpec as P


COL_GRP = ("col", "grp_0", "grp_1", "grp_2", "grp_3")
GRP = ("grp_0", "grp_1", "grp_2", "grp_3")
F32 = jnp.float32
BF16 = jnp.bfloat16

TAB = 64
ROWS = 16
LANES = 128
HALF = 64
EMB = 256
FEAT = 2336
WIDE = 2432
STEP = 8


def pieces():
    found = [(-1, 0, TAB, EMB)]
    place = EMB + TAB
    for row in range(TAB - 1):
        found.append((row, row + 1, TAB - 1 - row, place))
        place += TAB - 1 - row
    return found


def parts_of(place, count):
    found = []
    for tile in range(place // LANES, (place + count - 1) // LANES + 1):
        first = max(place, tile * LANES) - tile * LANES
        end = min(place + count, (tile + 1) * LANES) - tile * LANES
        found.append((tile, first, end))
    return found


def lane_iota(rows):
    return lax.broadcasted_iota(jnp.int32, (rows, LANES), 1)


def low_lanes(rows):
    return lane_iota(rows) < HALF


def turned(x, shift):
    shift %= LANES
    return x if shift == 0 else pltpu.roll(x, shift, 1)


def dot_t(a, b):
    return lax.dot_general(a, b, (((1,), (1,)), ((), ())), preferred_element_type=F32)


def hbm(shape, dtype):
    return pltpu.HBM(shape, dtype)


def vmem_specs(count):
    return [pl.BlockSpec(memory_space=pltpu.VMEM)] * count


def row_values():
    return lax.broadcasted_iota(jnp.int32, (256, LANES), 0).astype(F32).astype(BF16)


def counts_of(index_ref, length_ref, group, values):
    lanes = slice(group * LANES, (group + 1) * LANES)
    length = length_ref[0:1, lanes]
    one, none = jnp.ones((256, LANES), BF16), jnp.zeros((256, LANES), BF16)
    counts = none
    for slot in range(4):
        ids = jnp.where(slot < length, index_ref[0, slot : slot + 1, lanes], -1).astype(F32)
        ids = jnp.broadcast_to(ids, (16, LANES)).astype(BF16)
        counts = counts + jnp.where(jnp.concatenate([ids] * 16, axis=0) == values, one, none)
    return counts


def pool_kernel(index_ref, length_ref, rows_ref, out_ref):
    values = row_values()
    low = low_lanes(HALF)
    right = jnp.concatenate([rows_ref[0], rows_ref[0]], axis=0)
    for group in range(STEP):
        counts = counts_of(index_ref, length_ref, group, values)
        pooled = lax.dot_general(
            counts, right, (((0,), (1,)), ((), ())), preferred_element_type=F32
        )
        pooled = jnp.where(low, pooled[0:HALF], pooled[HALF:LANES]).astype(BF16)
        for peer in range(4):
            out_ref[peer, group] = pooled[peer * ROWS : (peer + 1) * ROWS]


def in_hbm(*arrays):
    return [pltpu.with_memory_space_constraint(x, pltpu.HBM) for x in arrays]


def pool(pool_index, bag_length, rows):
    return pl.pallas_call(
        pool_kernel,
        grid=(TAB // STEP,),
        in_specs=[
            pl.BlockSpec((1, 4, STEP * LANES), lambda i: (0, 0, i)),
            pl.BlockSpec((1, STEP * LANES), lambda i: (0, i)),
            pl.BlockSpec((1, HALF, 256), lambda i: (0, 0, 0)),
        ],
        out_specs=pl.BlockSpec((4, STEP, ROWS, LANES), lambda i: (0, i, 0, 0)),
        out_shape=hbm((4, TAB, ROWS, LANES), BF16),
        compiler_params=pltpu.CompilerParams(vmem_limit_bytes=12 << 20),
        name="pool",
    )(*in_hbm(pool_index, bag_length, rows))


def packed_bottom(mine_ref):
    low = low_lanes(ROWS)
    tiles = []
    for pair in range(2):
        lanes = slice(pair * LANES, (pair + 1) * LANES)
        first, second = mine_ref[0:ROWS, lanes], mine_ref[ROWS : 2 * ROWS, lanes]
        tiles.append(jnp.where(low, first, turned(second, HALF)))
        tiles.append(jnp.where(low, turned(first, HALF), second))
    return jnp.concatenate(tiles, axis=1)


def interact_kernel(slot_ref, arrived_ref, mine_ref, out_ref, vectors_ref, spaced, gram, edge):
    def place(table, carry):
        start = pl.multiple_of(slot_ref[table] * ROWS, ROWS)
        for part in range(4):
            spaced[part, pl.ds(start, ROWS), :] = arrived_ref[part, table].astype(F32)
        return carry

    lax.fori_loop(0, TAB, place, 0, unroll=8)
    bottom = packed_bottom(mine_ref)
    low = jnp.concatenate([low_lanes(TAB)] * 4, axis=1)
    for row in range(ROWS):
        vectors = jnp.concatenate(
            [spaced[part, pl.ds(row, TAB, stride=ROWS), :] for part in range(4)], axis=1
        )
        narrow = vectors.astype(BF16)
        vectors_ref[row] = narrow
        right = jnp.concatenate(
            [jnp.where(low, vectors, 0.0), jnp.where(low, 0.0, vectors)], axis=0
        ).astype(BF16)
        extra = jnp.broadcast_to(bottom[row : row + 1], (ROWS, 512)).astype(BF16)
        product = dot_t(jnp.concatenate([narrow, extra], axis=0), right)
        gram[pl.ds(row, TAB, stride=ROWS), :] = product[0:TAB]
        edge[row : row + 1, :] = product[TAB : TAB + 1]

    lane = lane_iota(ROWS)
    for half in range(2):
        where = slice(half * ROWS, (half + 1) * ROWS)
        out_ref[where, 0:EMB] = mine_ref[where, :].astype(BF16)
        tile, filled = EMB // LANES, jnp.zeros((ROWS, LANES), F32)
        for row, start, count, spot in pieces():
            source = edge[...] if row < 0 else gram[row * ROWS : (row + 1) * ROWS, :]
            moved = turned(source, spot - start - half * HALF)
            for at, first, end in parts_of(spot, count):
                if at != tile:
                    out_ref[where, tile * LANES : (tile + 1) * LANES] = filled.astype(BF16)
                    tile, filled = at, jnp.zeros((ROWS, LANES), F32)
                filled = jnp.where((lane >= first) & (lane < end), moved, filled)
        out_ref[where, tile * LANES : (tile + 1) * LANES] = filled.astype(BF16)


def interact(table_slot, arrived, mine):
    return pl.pallas_call(
        interact_kernel,
        in_specs=[
            pl.BlockSpec(memory_space=pltpu.SMEM),
            pl.BlockSpec(memory_space=pltpu.VMEM),
            pl.BlockSpec(memory_space=pltpu.VMEM),
        ],
        out_specs=[pl.BlockSpec(memory_space=pltpu.VMEM)] * 2,
        out_shape=[
            jax.ShapeDtypeStruct((2 * ROWS, WIDE), BF16),
            hbm((ROWS, TAB, 512), BF16),
        ],
        scratch_shapes=[
            pltpu.VMEM((4, TAB * ROWS, LANES), F32),
            pltpu.VMEM((TAB * ROWS, LANES), F32),
            pltpu.VMEM((ROWS, LANES), F32),
        ],
        compiler_params=pltpu.CompilerParams(vmem_limit_bytes=16 << 20),
        name="interact",
    )(table_slot, arrived, mine)


def top_kernel(
    f0, f1, f2, f3, weight_ref, out_weight_ref,
    all_ref, z0, z1, z2, z3, partial_ref, delta_ref, hidden_ref,
):
    for part, ref in enumerate((f0, f1, f2, f3)):
        all_ref[part * 32 : (part + 1) * 32, :] = ref[...]
    weight = weight_ref[...]
    pre = jnp.dot(all_ref[:, 0:FEAT], weight, preferred_element_type=F32)
    sigma = jax.nn.sigmoid(pre)
    hidden = (pre * sigma).astype(BF16)
    slope = sigma * (1.0 + pre * (1.0 - sigma))
    out_weight = out_weight_ref[0:1, :]
    delta = (out_weight * slope).astype(BF16)
    hidden_ref[...] = hidden
    delta_ref[...] = delta
    partial_ref[...] = dot_t(jnp.broadcast_to(out_weight, (16, 512)).astype(BF16), hidden)[0:8]
    z = dot_t(delta, weight).astype(BF16)
    for part, ref in enumerate((z0, z1, z2, z3)):
        ref[:, 0:FEAT] = z[part * 32 : (part + 1) * 32]
        ref[:, FEAT:WIDE] = jnp.zeros((32, WIDE - FEAT), BF16)


def top(parts, top_weight, out_weight):
    return pl.pallas_call(
        top_kernel,
        in_specs=vmem_specs(6),
        out_specs=vmem_specs(8),
        out_shape=[hbm((128, WIDE), BF16), hbm((32, WIDE), BF16)]
        + [jax.ShapeDtypeStruct((32, WIDE), BF16)] * 3
        + [
            jax.ShapeDtypeStruct((8, LANES), F32),
            hbm((128, 512), BF16),
            hbm((128, 512), BF16),
        ],
        compiler_params=pltpu.CompilerParams(vmem_limit_bytes=24 << 20),
        name="top",
    )(*parts, top_weight, out_weight)


def weight_grad_kernel(
    core_ref, p0, p1, p2, p3, labels_ref, all_ref, delta_ref, hidden_ref,
    own_ref, other_ref, logit_ref, dlogit_ref, grad,
):
    logits = (p0[...] + turned(p2[...], 64)) + (turned(p1[...], 32) + turned(p3[...], 96))
    logit_ref[...] = logits
    dlogit = (jax.nn.sigmoid(logits) - labels_ref[0:1, :]) * (1.0 / 128.0)
    dlogit_ref[...] = dlogit
    column = dlogit.T[:, 0:1]
    delta = (delta_ref[...].astype(F32) * column).astype(BF16)
    last = WIDE - LANES
    grad[:, 0:last] = lax.dot_general(
        delta, all_ref[:, 0:last], (((0,), (0,)), ((), ())), preferred_element_type=F32
    )
    lane = lane_iota(128)
    coarse = column.astype(BF16).astype(F32)
    spots = jnp.where(lane == 32, coarse, jnp.where(lane == 33, column - coarse, 0.0)).astype(BF16)
    grad[:, last:WIDE] = lax.dot_general(
        jnp.concatenate([delta, hidden_ref[...]], axis=0),
        jnp.concatenate([all_ref[:, last:WIDE], spots], axis=0),
        (((0,), (0,)), ((), ())),
        preferred_element_type=F32,
    )
    core = core_ref[0]
    for x in range(4):
        for y in range(4):
            for ref, which in ((own_ref, core), (other_ref, 1 - core)):
                both = []
                for z in range(2):
                    first = pl.multiple_of((((x * 2 + z) * 4 + y) * 2 + which) * 8, 8)
                    both.append(grad[pl.ds(first, 8), :])
                ref[x * 4 + y] = jnp.concatenate(both, axis=0).astype(BF16)


def weight_grad(core, partials, labels, features, delta, hidden):
    return pl.pallas_call(
        weight_grad_kernel,
        in_specs=[pl.BlockSpec(memory_space=pltpu.SMEM)] + vmem_specs(8),
        out_specs=vmem_specs(4),
        out_shape=[
            hbm((16, 16, WIDE), BF16),
            hbm((16, 16, WIDE), BF16),
            jax.ShapeDtypeStruct((8, LANES), F32),
            jax.ShapeDtypeStruct((8, LANES), F32),
        ],
        scratch_shapes=[pltpu.VMEM((512, WIDE), F32)],
        compiler_params=pltpu.CompilerParams(vmem_limit_bytes=32 << 20),
        name="weight_grad",
    )(core, *partials, labels, *in_hbm(features, delta, hidden))


def spread_kernel(
    slot_ref, z0, z1, z2, z3, dlogit_ref, vectors_ref, mine_ref, slope_ref, dense_ref,
    back_ref, bottom_ref, dfeat, upper, edge, right, dvec, dedge,
):
    column = dlogit_ref[...].T[0:32, 0:1]
    summed = z0[...].astype(F32) + z1[...].astype(F32) + z2[...].astype(F32) + z3[...].astype(F32)
    dfeat[...] = summed * column
    lane = lane_iota(ROWS)
    for row, start, count, spot in pieces():
        filled = jnp.zeros((ROWS, LANES), F32)
        for half in range(2):
            for at, first, end in parts_of(spot, count):
                source = dfeat[half * ROWS : (half + 1) * ROWS, at * LANES : (at + 1) * LANES]
                moved = turned(source, start + half * HALF - spot)
                shift = start + half * HALF - spot + at * LANES
                inside = (lane >= first + shift) & (lane < end + shift)
                filled = jnp.where(inside, moved, filled)
        filled = filled.astype(BF16).astype(F32)
        if row < 0:
            edge[...] = filled
        else:
            upper[row * ROWS : (row + 1) * ROWS, :] = filled
    upper[(TAB - 1) * ROWS :, :] = jnp.zeros((ROWS, LANES), F32)
    right[...] = jnp.zeros_like(right)
    bottom = packed_bottom(mine_ref)
    low = low_lanes(TAB)
    low_wide = jnp.concatenate([low] * 4, axis=1)
    low_few = jnp.concatenate([low_lanes(16)] * 4, axis=1)
    top_row = lax.broadcasted_iota(jnp.int32, (16, 512), 0) == 0
    for row in range(ROWS):
        half = upper[pl.ds(row, TAB, stride=ROWS), :]
        zeroth = jnp.broadcast_to(edge[row : row + 1, :], (TAB, LANES))
        flipped = jnp.concatenate([half, zeroth], axis=0).T
        first, second = flipped[0:TAB], turned(flipped[TAB : 2 * TAB], HALF)
        whole_matrix = half + jnp.where(low, first, second)
        edges = jnp.where(low, second, first)
        left = jnp.concatenate(
            [
                jnp.concatenate([whole_matrix, edges], axis=1),
                jnp.concatenate([zeroth[0:16], jnp.zeros((16, LANES), F32)], axis=1),
            ],
            axis=0,
        ).astype(BF16)
        vectors = vectors_ref[row].astype(F32)
        right[0:TAB, :] = jnp.where(low_wide, vectors, 0.0).astype(BF16)
        right[TAB : 2 * TAB, :] = jnp.where(low_wide, 0.0, vectors).astype(BF16)
        own = jnp.broadcast_to(bottom[row : row + 1], (16, 512))
        right[128:144, :] = jnp.where(top_row & ~low_few, own, 0.0).astype(BF16)
        right[192:208, :] = jnp.where(top_row & low_few, own, 0.0).astype(BF16)
        product = jnp.dot(left, right[...], preferred_element_type=F32)
        for part in range(4):
            lanes = slice(part * LANES, (part + 1) * LANES)
            dvec[part, pl.ds(row, TAB, stride=ROWS), :] = product[0:TAB, lanes]
        dedge[row : row + 1, :] = product[TAB : TAB + 1]

    def place(table, carry):
        start = pl.multiple_of(slot_ref[table] * ROWS, ROWS)
        for part in range(4):
            back_ref[part, table] = dvec[part, pl.ds(start, ROWS), :].astype(BF16)
        return carry

    lax.fori_loop(0, TAB, place, 0, unroll=8)
    low = low_lanes(ROWS)
    tiles = [dedge[:, part * LANES : (part + 1) * LANES] for part in range(4)]
    own_rows = [
        jnp.concatenate(
            [jnp.where(low, tiles[2 * p], turned(tiles[2 * p + 1], HALF)) for p in range(2)], axis=1
        ),
        jnp.concatenate(
            [jnp.where(low, turned(tiles[2 * p], HALF), tiles[2 * p + 1]) for p in range(2)], axis=1
        ),
    ]
    dbottom = (dfeat[:, 0:EMB] + jnp.concatenate(own_rows, axis=0)) * slope_ref[...]
    bottom_ref[...] = lax.dot_general(
        dense_ref[...],
        dbottom,
        (((0,), (0,)), ((), ())),
        precision=lax.Precision.HIGHEST,
        preferred_element_type=F32,
    )


def spread(table_slot, zs, dlogit, vectors, mine, slope, dense):
    return pl.pallas_call(
        spread_kernel,
        in_specs=[pl.BlockSpec(memory_space=pltpu.SMEM)]
        + [pl.BlockSpec(memory_space=pltpu.VMEM)] * 9,
        out_specs=[pl.BlockSpec(memory_space=pltpu.VMEM)] * 2,
        out_shape=[
            hbm((4, TAB, ROWS, LANES), BF16),
            jax.ShapeDtypeStruct((16, EMB), F32),
        ],
        scratch_shapes=[
            pltpu.VMEM((2 * ROWS, WIDE), F32),
            pltpu.VMEM((TAB * ROWS, LANES), F32),
            pltpu.VMEM((ROWS, LANES), F32),
            pltpu.VMEM((256, 512), BF16),
            pltpu.VMEM((4, TAB * ROWS, LANES), F32),
            pltpu.VMEM((ROWS, 512), F32),
        ],
        compiler_params=pltpu.CompilerParams(vmem_limit_bytes=16 << 20),
        name="spread",
    )(table_slot, *zs, dlogit, vectors, mine, slope, dense)


def row_grad_kernel(index_ref, length_ref, back_ref, out_ref, total, counted, moved):
    step = pl.program_id(0)

    @pl.when(step == 0)
    def _():
        total[...] = jnp.zeros_like(total)

    values = row_values()
    low = low_lanes(HALF)
    first = jnp.where(low, 1.0, 0.0).astype(BF16)
    second = jnp.where(low, 0.0, 1.0).astype(BF16)
    for group in range(STEP):
        lanes = slice(group * LANES, (group + 1) * LANES)
        counted[:, lanes] = counts_of(index_ref, length_ref, group, values)
        rows = jnp.concatenate([back_ref[peer, group] for peer in range(4)], axis=0)
        moved[group * LANES : group * LANES + HALF, :] = rows * first
        moved[group * LANES + HALF : (group + 1) * LANES, :] = rows * second
    total[...] += jnp.dot(counted[...], moved[...], preferred_element_type=F32)

    @pl.when(step == pl.num_programs(0) - 1)
    def _():
        flipped = total[...].T
        out_ref[0] = flipped[0:HALF] + flipped[HALF:LANES]


def row_grad(pool_index, bag_length, back):
    return pl.pallas_call(
        row_grad_kernel,
        grid=(TAB // STEP,),
        in_specs=[
            pl.BlockSpec((1, 4, STEP * LANES), lambda i: (0, 0, i)),
            pl.BlockSpec((1, STEP * LANES), lambda i: (0, i)),
            pl.BlockSpec((4, STEP, ROWS, LANES), lambda i: (0, i, 0, 0)),
        ],
        out_specs=pl.BlockSpec((1, HALF, 256), lambda i: (0, 0, 0)),
        out_shape=jax.ShapeDtypeStruct((1, HALF, 256), F32),
        scratch_shapes=[
            pltpu.VMEM((256, LANES), F32),
            pltpu.VMEM((256, STEP * LANES), BF16),
            pltpu.VMEM((STEP * LANES, LANES), BF16),
        ],
        compiler_params=pltpu.CompilerParams(vmem_limit_bytes=12 << 20),
        name="row_grad",
    )(*in_hbm(pool_index, bag_length), back)


def shifted(x, axis, shift):
    size = lax.axis_size(axis)
    return lax.ppermute(x, axis, [(i, (i + shift) % size) for i in range(size)])


def exchange_all(x):
    flat = x.reshape(4 * TAB, ROWS, LANES)
    flat = lax.all_to_all(flat, COL_GRP, split_axis=0, concat_axis=0, tiled=True)
    return flat.reshape(4, TAB, ROWS, LANES)


def summed_over(x, axis):
    if lax.axis_size(axis) == 2:
        return x + shifted(x, axis, 1)
    others = [shifted(x, axis, shift) for shift in (1, 2, 3)]
    return (x + others[1]) + (others[0] + others[2])


def split(x):
    high = x.astype(BF16)
    return high, (x - high.astype(F32)).astype(BF16)


def reduced_to(x, axis, shared=None):
    me = lax.axis_index(axis)
    size = lax.axis_size(axis)
    total = lax.dynamic_index_in_dim(x, me, 0, keepdims=False).astype(F32)
    rows, width = total.shape
    if shared is not None:
        high, low = split(shared)
        own = high.astype(F32) + low.astype(F32)
        cuts = [v[r : r + rows] for v in (high, low) for r in range(0, shared.shape[0], rows)]
    others = []
    for shift in range(1, size):
        block = lax.dynamic_index_in_dim(x, (me + shift) % size, 0, keepdims=False).astype(BF16)
        if shared is not None:
            block = jnp.concatenate([block, *cuts], axis=1)
        block = shifted(block, axis, shift).astype(F32)
        total = total + block[:, 0:width]
        if shared is not None:
            wide = shared.shape[1]
            parts = [block[:, p : p + wide] for p in range(width, block.shape[1], wide)]
            half = len(parts) // 2
            others.append(jnp.concatenate([a + b for a, b in zip(parts[:half], parts[half:])], axis=0))
    if shared is None:
        return total
    if size == 2:
        return total, own + others[0]
    return total, (own + others[1]) + (others[0] + others[2])


def silu_slope(values):
    sigma = jax.nn.sigmoid(values)
    return sigma * (1.0 + values * (1.0 - sigma))


def step(
    table_rows,
    pool_index,
    bag_length,
    table_slot,
    dense_input,
    bottom_weight,
    top_weight,
    out_weight,
    labels,
):
    me, core = lax.axis_index("col"), lax.axis_index("grp_3")
    rows = jnp.transpose(table_rows, (0, 2, 1))
    pooled = pool(pool_index, bag_length, rows)
    arrived = exchange_all(pooled)

    dense_mine = lax.dynamic_index_in_dim(
        dense_input.reshape(2, 4, ROWS, -1), me, 1, keepdims=False
    ).reshape(2 * ROWS, -1)
    mine_pre = jnp.dot(dense_mine, bottom_weight, preferred_element_type=F32)
    mine = jax.nn.silu(mine_pre).astype(BF16).astype(F32)
    mine_slope = silu_slope(mine_pre)
    dense_wide = jnp.pad(dense_mine.astype(F32), ((0, 0), (0, 16 - dense_mine.shape[1])))
    order = (me - jnp.arange(4)) % 4
    labels_rel = jnp.take(
        jnp.transpose(labels.reshape(2, 4, ROWS), (1, 0, 2)), order, axis=0
    ).reshape(1, LANES).astype(F32)
    out_weight_row = out_weight.astype(F32).reshape(1, -1)

    part, vectors = interact(table_slot, arrived, mine)
    parts = [part] + [shifted(part, "col", away) for away in (1, 2, 3)]
    features, *zs, partial, delta, hidden = top(parts, top_weight, out_weight_row)
    zs = [zs[0]] + [shifted(zs[away], "col", -away) for away in (1, 2, 3)]
    partials = [partial] + [shifted(partial, "col", away) for away in (1, 2, 3)]
    own, other, logits_rel, dlogit = weight_grad(
        core.astype(jnp.int32).reshape(1), partials, labels_rel, features, delta, hidden
    )
    back, bottom = spread(table_slot, zs, dlogit, vectors, mine, mine_slope, dense_wide)
    returned = exchange_all(back)
    grad_rows = jnp.transpose(row_grad(pool_index, bag_length, returned), (0, 2, 1))

    logits = jnp.take(logits_rel[0].reshape(4, 2, ROWS), order, axis=0)
    logits = jnp.transpose(logits, (1, 0, 2)).reshape(LANES)

    other = shifted(other, "grp_3", 1)
    grad = (own.astype(F32) + other.astype(F32)).astype(BF16).reshape(4, 64, WIDE)
    grad = reduced_to(grad, "grp_0").reshape(4, 16, WIDE)
    for axis in ("grp_3", "grp_0"):
        bottom = summed_over(bottom, axis)
    grad, bottom = reduced_to(grad, "grp_2", bottom)
    grad, bottom = reduced_to(grad.reshape(2, 8, WIDE), "grp_1", bottom)
    grad_top = jnp.transpose(grad[:, 0:FEAT])
    grad_out = grad[:, FEAT] + grad[:, FEAT + 1]
    grad_bottom = summed_over(bottom, "col")[0 : bottom_weight.shape[0]]
    return (logits, grad_top, grad_out, grad_bottom, grad_rows)


def solution(mesh):
    torus = Mesh(
        mesh.devices.reshape(mesh.shape["col"], 4, 2, 4, 2),
        ("col", "grp_0", "grp_1", "grp_2", "grp_3"),
    )
    return jax.shard_map(
        step,
        mesh=torus,
        in_specs=(
            P(GRP, None, "col"),
            P(GRP, None, None),
            P(GRP, None),
            P(),
            P(GRP, None),
            P(),
            P(None, "col"),
            P("col"),
            P(GRP),
        ),
        out_specs=(P(GRP), P(None, COL_GRP), P(COL_GRP), P(), P(GRP, None, "col")),
        check_vma=False,
    )
```

```python
import jax
import jax.numpy as jnp
from jax import lax
from jax.experimental import pallas as pl
from jax.experimental.pallas import tpu as pltpu
from jax.sharding import Mesh
from jax.sharding import PartitionSpec as P


COL_GRP = ("col", "grp_0", "grp_1", "grp_2", "grp_3")
GRP = ("grp_0", "grp_1", "grp_2", "grp_3")
F32 = jnp.float32
BF16 = jnp.bfloat16

TAB = 64
ROWS = 16
LANES = 128
HALF = 64
EMB = 256
FEAT = 2336
WIDE = 2432
STEP = 8
LABEL_LANE = 36


def pieces():
    found = [(-1, 0, TAB, EMB)]
    place = EMB + TAB
    for row in range(TAB - 1):
        found.append((row, row + 1, TAB - 1 - row, place))
        place += TAB - 1 - row
    return found


def parts_of(place, count):
    found = []
    for tile in range(place // LANES, (place + count - 1) // LANES + 1):
        first = max(place, tile * LANES) - tile * LANES
        end = min(place + count, (tile + 1) * LANES) - tile * LANES
        found.append((tile, first, end))
    return found


def lane_iota(rows):
    return lax.broadcasted_iota(jnp.int32, (rows, LANES), 1)


def low_lanes(rows):
    return lane_iota(rows) < HALF


def turned(x, shift):
    shift %= LANES
    return x if shift == 0 else pltpu.roll(x, shift, 1)


def dot_t(a, b):
    return lax.dot_general(a, b, (((1,), (1,)), ((), ())), preferred_element_type=F32)


def hbm(shape, dtype):
    return pltpu.HBM(shape, dtype)


def vmem_specs(count):
    return [pl.BlockSpec(memory_space=pltpu.VMEM)] * count


def row_values():
    return lax.broadcasted_iota(jnp.int32, (256, LANES), 0).astype(F32).astype(BF16)


def counts_of(index_ref, length_ref, group, values):
    lanes = slice(group * LANES, (group + 1) * LANES)
    length = length_ref[0:1, lanes]
    one, none = jnp.ones((256, LANES), BF16), jnp.zeros((256, LANES), BF16)
    counts = none
    for slot in range(4):
        ids = jnp.where(slot < length, index_ref[0, slot : slot + 1, lanes], -1).astype(F32)
        ids = jnp.broadcast_to(ids, (16, LANES)).astype(BF16)
        counts = counts + jnp.where(jnp.concatenate([ids] * 16, axis=0) == values, one, none)
    return counts


def pool_kernel(index_ref, length_ref, rows_ref, out_ref):
    values = row_values()
    low = low_lanes(HALF)
    right = jnp.concatenate([rows_ref[0], rows_ref[0]], axis=0)
    for group in range(STEP):
        counts = counts_of(index_ref, length_ref, group, values)
        pooled = lax.dot_general(
            counts, right, (((0,), (1,)), ((), ())), preferred_element_type=F32
        )
        pooled = jnp.where(low, pooled[0:HALF], pooled[HALF:LANES]).astype(BF16)
        for peer in range(4):
            out_ref[peer, group] = pooled[peer * ROWS : (peer + 1) * ROWS]


def in_hbm(*arrays):
    return [pltpu.with_memory_space_constraint(x, pltpu.HBM) for x in arrays]


def pool(pool_index, bag_length, rows):
    return pl.pallas_call(
        pool_kernel,
        grid=(TAB // STEP,),
        in_specs=[
            pl.BlockSpec((1, 4, STEP * LANES), lambda i: (0, 0, i)),
            pl.BlockSpec((1, STEP * LANES), lambda i: (0, i)),
            pl.BlockSpec((1, HALF, 256), lambda i: (0, 0, 0)),
        ],
        out_specs=pl.BlockSpec((4, STEP, ROWS, LANES), lambda i: (0, i, 0, 0)),
        out_shape=hbm((4, TAB, ROWS, LANES), BF16),
        compiler_params=pltpu.CompilerParams(vmem_limit_bytes=12 << 20),
        name="pool",
    )(*in_hbm(pool_index, bag_length, rows))


def packed_bottom(mine_ref):
    low = low_lanes(ROWS)
    tiles = []
    for pair in range(2):
        lanes = slice(pair * LANES, (pair + 1) * LANES)
        first, second = mine_ref[0:ROWS, lanes], mine_ref[ROWS : 2 * ROWS, lanes]
        tiles.append(jnp.where(low, first, turned(second, HALF)))
        tiles.append(jnp.where(low, turned(first, HALF), second))
    return jnp.concatenate(tiles, axis=1)


def interact_kernel(slot_ref, arrived_ref, mine_ref, label_ref, out_ref, vectors_ref, spaced, gram, edge):
    def place(table, carry):
        start = pl.multiple_of(slot_ref[table] * ROWS, ROWS)
        for part in range(4):
            spaced[part, pl.ds(start, ROWS), :] = arrived_ref[part, table].astype(F32)
        return carry

    lax.fori_loop(0, TAB, place, 0, unroll=8)
    bottom = packed_bottom(mine_ref)
    low = jnp.concatenate([low_lanes(TAB)] * 4, axis=1)
    for row in range(ROWS):
        vectors = jnp.concatenate(
            [spaced[part, pl.ds(row, TAB, stride=ROWS), :] for part in range(4)], axis=1
        )
        narrow = vectors.astype(BF16)
        vectors_ref[row] = narrow
        right = jnp.concatenate(
            [jnp.where(low, vectors, 0.0), jnp.where(low, 0.0, vectors)], axis=0
        ).astype(BF16)
        extra = jnp.broadcast_to(bottom[row : row + 1], (ROWS, 512)).astype(BF16)
        product = dot_t(jnp.concatenate([narrow, extra], axis=0), right)
        gram[pl.ds(row, TAB, stride=ROWS), :] = product[0:TAB]
        edge[row : row + 1, :] = product[TAB : TAB + 1]

    lane = lane_iota(ROWS)
    for half in range(2):
        where = slice(half * ROWS, (half + 1) * ROWS)
        out_ref[where, 0:EMB] = mine_ref[where, :].astype(BF16)
        tile, filled = EMB // LANES, jnp.zeros((ROWS, LANES), F32)
        for row, start, count, spot in pieces():
            source = edge[...] if row < 0 else gram[row * ROWS : (row + 1) * ROWS, :]
            moved = turned(source, spot - start - half * HALF)
            for at, first, end in parts_of(spot, count):
                if at != tile:
                    out_ref[where, tile * LANES : (tile + 1) * LANES] = filled.astype(BF16)
                    tile, filled = at, jnp.zeros((ROWS, LANES), F32)
                filled = jnp.where((lane >= first) & (lane < end), moved, filled)
        filled = jnp.where(lane == LABEL_LANE, label_ref[where, :], filled)
        out_ref[where, tile * LANES : (tile + 1) * LANES] = filled.astype(BF16)


def interact(table_slot, arrived, mine, labels):
    return pl.pallas_call(
        interact_kernel,
        in_specs=[
            pl.BlockSpec(memory_space=pltpu.SMEM),
            *vmem_specs(3),
        ],
        out_specs=[pl.BlockSpec(memory_space=pltpu.VMEM)] * 2,
        out_shape=[
            jax.ShapeDtypeStruct((2 * ROWS, WIDE), BF16),
            hbm((ROWS, TAB, 512), BF16),
        ],
        scratch_shapes=[
            pltpu.VMEM((4, TAB * ROWS, LANES), F32),
            pltpu.VMEM((TAB * ROWS, LANES), F32),
            pltpu.VMEM((ROWS, LANES), F32),
        ],
        compiler_params=pltpu.CompilerParams(vmem_limit_bytes=16 << 20),
        name="interact",
    )(table_slot, arrived, mine, labels)


def top_kernel(
    f0, f1, f2, f3, weight_ref, out_weight_ref,
    all_ref, z0, z1, z2, z3, partial_ref, delta_ref, hidden_ref,
):
    for part, ref in enumerate((f0, f1, f2, f3)):
        all_ref[part * 32 : (part + 1) * 32, :] = ref[...]
    weight = weight_ref[...]
    pre = jnp.dot(all_ref[:, 0:FEAT], weight, preferred_element_type=F32)
    sigma = jax.nn.sigmoid(pre)
    hidden = (pre * sigma).astype(BF16)
    slope = sigma * (1.0 + pre * (1.0 - sigma))
    out_weight = out_weight_ref[0:1, :]
    delta = (out_weight * slope).astype(BF16)
    hidden_ref[...] = hidden
    delta_ref[...] = delta
    partial_ref[...] = dot_t(jnp.broadcast_to(out_weight, (16, 512)).astype(BF16), hidden)[0:8]
    z = dot_t(delta, weight).astype(BF16)
    for part, ref in enumerate((z0, z1, z2, z3)):
        ref[:, 0:FEAT] = z[part * 32 : (part + 1) * 32]
        ref[:, FEAT:WIDE] = jnp.zeros((32, WIDE - FEAT), BF16)


def top(parts, top_weight, out_weight):
    return pl.pallas_call(
        top_kernel,
        in_specs=vmem_specs(6),
        out_specs=vmem_specs(8),
        out_shape=[hbm((128, WIDE), BF16), hbm((32, WIDE), BF16)]
        + [jax.ShapeDtypeStruct((32, WIDE), BF16)] * 3
        + [
            jax.ShapeDtypeStruct((8, LANES), F32),
            hbm((128, 512), BF16),
            hbm((128, 512), BF16),
        ],
        compiler_params=pltpu.CompilerParams(vmem_limit_bytes=24 << 20),
        name="top",
    )(*parts, top_weight, out_weight)


def own_logits(even, r0, up1, down1, up2, down2):
    return (r0 + turned(up1, -32)) + (turned(down1, -64) + turned(jnp.where(even, up2, down2), -96))


def weight_grad_kernel(
    place_ref, p0, p1, p2, p3, p4, p5, all_ref, delta_ref, hidden_ref, own_ref, other_ref, grad,
):
    even = place_ref[1] == 0
    r0, up1, down1, up2, down2, far = (p[...] for p in (p0, p1, p2, p3, p4, p5))

    def at(x, slot, to):
        return turned(x, 32 * (to - slot))

    own = own_logits(even, r0, up1, down1, up2, down2)
    below = at(down1, 0, 1) + r0 + at(down2, 2, 1) + at(jnp.where(even, far, up1), 3, 1)
    above = at(up1, 0, 2) + at(up2, 1, 2) + r0 + at(jnp.where(even, down1, far), 3, 2)
    across = r0 + jnp.where(
        even,
        at(down2, 0, 3) + at(down1, 1, 3) + at(far, 2, 3),
        at(up2, 0, 3) + at(far, 1, 3) + at(up1, 2, 3),
    )
    block = lane_iota(8) // 32
    logits = jnp.where(block == 0, own, jnp.where(block == 1, below, jnp.where(block == 2, above, across)))
    tile = all_ref[:, WIDE - LANES : WIDE].astype(F32)
    labels = jnp.sum(jnp.where(lane_iota(128) == LABEL_LANE, tile, 0.0), axis=1, keepdims=True)
    column = (jax.nn.sigmoid(logits.T[:, 0:1]) - labels) * (1.0 / 128.0)
    delta = (delta_ref[...].astype(F32) * column).astype(BF16)
    last = WIDE - LANES
    grad[:, 0:last] = lax.dot_general(
        delta, all_ref[:, 0:last], (((0,), (0,)), ((), ())), preferred_element_type=F32
    )
    lane = lane_iota(128)
    coarse = column.astype(BF16).astype(F32)
    spots = jnp.where(lane == 32, coarse, jnp.where(lane == 33, column - coarse, 0.0)).astype(BF16)
    grad[:, last:WIDE] = lax.dot_general(
        jnp.concatenate([delta, hidden_ref[...]], axis=0),
        jnp.concatenate([all_ref[:, last:WIDE], spots], axis=0),
        (((0,), (0,)), ((), ())),
        preferred_element_type=F32,
    )
    core = place_ref[0]
    for x in range(4):
        for y in range(4):
            for ref, which in ((own_ref, core), (other_ref, 1 - core)):
                both = []
                for z in range(2):
                    first = pl.multiple_of((((x * 2 + z) * 4 + y) * 2 + which) * 8, 8)
                    both.append(grad[pl.ds(first, 8), :])
                ref[x * 4 + y] = jnp.concatenate(both, axis=0).astype(BF16)


def weight_grad(place, partials, features, delta, hidden):
    return pl.pallas_call(
        weight_grad_kernel,
        in_specs=[pl.BlockSpec(memory_space=pltpu.SMEM)] + vmem_specs(9),
        out_specs=vmem_specs(2),
        out_shape=[
            hbm((16, 16, WIDE), BF16),
            hbm((16, 16, WIDE), BF16),
        ],
        scratch_shapes=[pltpu.VMEM((512, WIDE), F32)],
        compiler_params=pltpu.CompilerParams(vmem_limit_bytes=32 << 20),
        name="weight_grad",
    )(place, *partials, *in_hbm(features, delta, hidden))


def spread_kernel(
    slot_ref, place_ref, z0, z1, z2, z3, p0, p1, p2, p3, p4, label_ref, vectors_ref, mine_ref,
    slope_ref, dense_ref, back_ref, bottom_ref, logit_ref, dfeat, upper, edge, right, dvec, dedge,
):
    logits = own_logits(place_ref[1] == 0, p0[...], p1[...], p2[...], p3[...], p4[...])
    logit_ref[...] = logits
    labels = jnp.sum(jnp.where(lane_iota(32) == LABEL_LANE, label_ref[...], 0.0), axis=1, keepdims=True)
    column = (jax.nn.sigmoid(logits.T[0:32, 0:1]) - labels) * (1.0 / 128.0)
    summed = z0[...].astype(F32) + z1[...].astype(F32) + z2[...].astype(F32) + z3[...].astype(F32)
    dfeat[...] = summed * column
    lane = lane_iota(ROWS)
    for row, start, count, spot in pieces():
        filled = jnp.zeros((ROWS, LANES), F32)
        for half in range(2):
            for at, first, end in parts_of(spot, count):
                source = dfeat[half * ROWS : (half + 1) * ROWS, at * LANES : (at + 1) * LANES]
                moved = turned(source, start + half * HALF - spot)
                shift = start + half * HALF - spot + at * LANES
                inside = (lane >= first + shift) & (lane < end + shift)
                filled = jnp.where(inside, moved, filled)
        filled = filled.astype(BF16).astype(F32)
        if row < 0:
            edge[...] = filled
        else:
            upper[row * ROWS : (row + 1) * ROWS, :] = filled
    upper[(TAB - 1) * ROWS :, :] = jnp.zeros((ROWS, LANES), F32)
    right[...] = jnp.zeros_like(right)
    bottom = packed_bottom(mine_ref)
    low = low_lanes(TAB)
    low_wide = jnp.concatenate([low] * 4, axis=1)
    low_few = jnp.concatenate([low_lanes(16)] * 4, axis=1)
    top_row = lax.broadcasted_iota(jnp.int32, (16, 512), 0) == 0
    for row in range(ROWS):
        half = upper[pl.ds(row, TAB, stride=ROWS), :]
        zeroth = jnp.broadcast_to(edge[row : row + 1, :], (TAB, LANES))
        flipped = jnp.concatenate([half, zeroth], axis=0).T
        first, second = flipped[0:TAB], turned(flipped[TAB : 2 * TAB], HALF)
        whole_matrix = half + jnp.where(low, first, second)
        edges = jnp.where(low, second, first)
        left = jnp.concatenate(
            [
                jnp.concatenate([whole_matrix, edges], axis=1),
                jnp.concatenate([zeroth[0:16], jnp.zeros((16, LANES), F32)], axis=1),
            ],
            axis=0,
        ).astype(BF16)
        vectors = vectors_ref[row].astype(F32)
        right[0:TAB, :] = jnp.where(low_wide, vectors, 0.0).astype(BF16)
        right[TAB : 2 * TAB, :] = jnp.where(low_wide, 0.0, vectors).astype(BF16)
        own = jnp.broadcast_to(bottom[row : row + 1], (16, 512))
        right[128:144, :] = jnp.where(top_row & ~low_few, own, 0.0).astype(BF16)
        right[192:208, :] = jnp.where(top_row & low_few, own, 0.0).astype(BF16)
        product = jnp.dot(left, right[...], preferred_element_type=F32)
        for part in range(4):
            lanes = slice(part * LANES, (part + 1) * LANES)
            dvec[part, pl.ds(row, TAB, stride=ROWS), :] = product[0:TAB, lanes]
        dedge[row : row + 1, :] = product[TAB : TAB + 1]

    def place(table, carry):
        start = pl.multiple_of(slot_ref[table] * ROWS, ROWS)
        for part in range(4):
            back_ref[part, table] = dvec[part, pl.ds(start, ROWS), :].astype(BF16)
        return carry

    lax.fori_loop(0, TAB, place, 0, unroll=8)
    low = low_lanes(ROWS)
    tiles = [dedge[:, part * LANES : (part + 1) * LANES] for part in range(4)]
    own_rows = [
        jnp.concatenate(
            [jnp.where(low, tiles[2 * p], turned(tiles[2 * p + 1], HALF)) for p in range(2)], axis=1
        ),
        jnp.concatenate(
            [jnp.where(low, turned(tiles[2 * p], HALF), tiles[2 * p + 1]) for p in range(2)], axis=1
        ),
    ]
    dbottom = (dfeat[:, 0:EMB] + jnp.concatenate(own_rows, axis=0)) * slope_ref[...]
    bottom_ref[...] = lax.dot_general(
        dense_ref[...],
        dbottom,
        (((0,), (0,)), ((), ())),
        precision=lax.Precision.HIGHEST,
        preferred_element_type=F32,
    )


def spread(table_slot, place, zs, partials, labels, vectors, mine, slope, dense):
    return pl.pallas_call(
        spread_kernel,
        in_specs=[pl.BlockSpec(memory_space=pltpu.SMEM)] * 2 + vmem_specs(14),
        out_specs=vmem_specs(3),
        out_shape=[
            hbm((4, TAB, ROWS, LANES), BF16),
            jax.ShapeDtypeStruct((16, EMB), F32),
            jax.ShapeDtypeStruct((8, LANES), F32),
        ],
        scratch_shapes=[
            pltpu.VMEM((2 * ROWS, WIDE), F32),
            pltpu.VMEM((TAB * ROWS, LANES), F32),
            pltpu.VMEM((ROWS, LANES), F32),
            pltpu.VMEM((256, 512), BF16),
            pltpu.VMEM((4, TAB * ROWS, LANES), F32),
            pltpu.VMEM((ROWS, 512), F32),
        ],
        compiler_params=pltpu.CompilerParams(vmem_limit_bytes=16 << 20),
        name="spread",
    )(table_slot, place, *zs, *partials, labels, *in_hbm(vectors), mine, slope, dense)


def row_grad_kernel(index_ref, length_ref, back_ref, out_ref, total, counted, moved):
    step = pl.program_id(0)

    @pl.when(step == 0)
    def _():
        total[...] = jnp.zeros_like(total)

    values = row_values()
    low = low_lanes(HALF)
    first = jnp.where(low, 1.0, 0.0).astype(BF16)
    second = jnp.where(low, 0.0, 1.0).astype(BF16)
    for group in range(STEP):
        lanes = slice(group * LANES, (group + 1) * LANES)
        counted[:, lanes] = counts_of(index_ref, length_ref, group, values)
        rows = jnp.concatenate([back_ref[peer, group] for peer in range(4)], axis=0)
        moved[group * LANES : group * LANES + HALF, :] = rows * first
        moved[group * LANES + HALF : (group + 1) * LANES, :] = rows * second
    total[...] += jnp.dot(counted[...], moved[...], preferred_element_type=F32)

    @pl.when(step == pl.num_programs(0) - 1)
    def _():
        flipped = total[...].T
        out_ref[0] = flipped[0:HALF] + flipped[HALF:LANES]


def row_grad(pool_index, bag_length, back):
    return pl.pallas_call(
        row_grad_kernel,
        grid=(TAB // STEP,),
        in_specs=[
            pl.BlockSpec((1, 4, STEP * LANES), lambda i: (0, 0, i)),
            pl.BlockSpec((1, STEP * LANES), lambda i: (0, i)),
            pl.BlockSpec((4, STEP, ROWS, LANES), lambda i: (0, i, 0, 0)),
        ],
        out_specs=pl.BlockSpec((1, HALF, 256), lambda i: (0, 0, 0)),
        out_shape=jax.ShapeDtypeStruct((1, HALF, 256), F32),
        scratch_shapes=[
            pltpu.VMEM((256, LANES), F32),
            pltpu.VMEM((256, STEP * LANES), BF16),
            pltpu.VMEM((STEP * LANES, LANES), BF16),
        ],
        compiler_params=pltpu.CompilerParams(vmem_limit_bytes=12 << 20),
        name="row_grad",
    )(*in_hbm(pool_index, bag_length), back)


def shifted(x, axis, shift):
    size = lax.axis_size(axis)
    return lax.ppermute(x, axis, [(i, (i + shift) % size) for i in range(size)])


def ring_sent(x, moves):
    def spot(place):
        return place % 4 * 2 + place % 8 // 4

    pairs = [(spot(p), spot(p + moves(p))) for p in range(8)]
    return lax.ppermute(x, ("col", "grp_1"), pairs)


def exchange_all(x):
    flat = x.reshape(4 * TAB, ROWS, LANES)
    flat = lax.all_to_all(flat, COL_GRP, split_axis=0, concat_axis=0, tiled=True)
    return flat.reshape(4, TAB, ROWS, LANES)


def summed_over(x, axis):
    if lax.axis_size(axis) == 2:
        return x + shifted(x, axis, 1)
    others = [shifted(x, axis, shift) for shift in (1, 2, 3)]
    return (x + others[1]) + (others[0] + others[2])


def split(x):
    high = x.astype(BF16)
    return high, (x - high.astype(F32)).astype(BF16)


def reduced_to(x, axis, shared=None):
    me = lax.axis_index(axis)
    size = lax.axis_size(axis)
    total = lax.dynamic_index_in_dim(x, me, 0, keepdims=False).astype(F32)
    rows, width = total.shape
    if shared is not None:
        high, low = split(shared)
        own = high.astype(F32) + low.astype(F32)
        cuts = [v[r : r + rows] for v in (high, low) for r in range(0, shared.shape[0], rows)]
    others = []
    for shift in range(1, size):
        block = lax.dynamic_index_in_dim(x, (me + shift) % size, 0, keepdims=False).astype(BF16)
        if shared is not None:
            block = jnp.concatenate([block, *cuts], axis=1)
        block = shifted(block, axis, shift).astype(F32)
        total = total + block[:, 0:width]
        if shared is not None:
            wide = shared.shape[1]
            parts = [block[:, p : p + wide] for p in range(width, block.shape[1], wide)]
            half = len(parts) // 2
            others.append(jnp.concatenate([a + b for a, b in zip(parts[:half], parts[half:])], axis=0))
    if shared is None:
        return total
    if size == 2:
        return total, own + others[0]
    return total, (own + others[1]) + (others[0] + others[2])


def silu_slope(values):
    sigma = jax.nn.sigmoid(values)
    return sigma * (1.0 + values * (1.0 - sigma))


def step(
    table_rows,
    pool_index,
    bag_length,
    table_slot,
    dense_input,
    bottom_weight,
    top_weight,
    out_weight,
    labels,
):
    me, core = lax.axis_index("col"), lax.axis_index("grp_3")
    rows = jnp.transpose(table_rows, (0, 2, 1))
    pooled = pool(pool_index, bag_length, rows)
    arrived = exchange_all(pooled)

    dense_mine = lax.dynamic_index_in_dim(
        dense_input.reshape(2, 4, ROWS, -1), me, 1, keepdims=False
    ).reshape(2 * ROWS, -1)
    mine_pre = jnp.dot(dense_mine, bottom_weight, preferred_element_type=F32)
    mine = jax.nn.silu(mine_pre).astype(BF16).astype(F32)
    mine_slope = silu_slope(mine_pre)
    dense_wide = jnp.pad(dense_mine.astype(F32), ((0, 0), (0, 16 - dense_mine.shape[1])))
    labels_mine = lax.dynamic_index_in_dim(labels.reshape(2, 4, ROWS), me, 1, keepdims=False)
    labels_mine = jnp.broadcast_to(labels_mine.astype(F32).reshape(2 * ROWS, 1), (2 * ROWS, LANES))
    place = jnp.stack([core, me % 2]).astype(jnp.int32)
    out_weight_row = out_weight.astype(F32).reshape(1, -1)

    part, vectors = interact(table_slot, arrived, mine, labels_mine)
    parts = [
        part,
        ring_sent(part, lambda p: 1),
        ring_sent(part, lambda p: -1),
        ring_sent(part, lambda p: -2 if p % 2 else 2),
    ]
    features, *zs, partial, delta, hidden = top(parts, top_weight, out_weight_row)
    zs = [
        zs[0],
        ring_sent(zs[1], lambda p: -1),
        ring_sent(zs[2], lambda p: 1),
        ring_sent(zs[3], lambda p: 2 if p % 2 else -2),
    ]
    partials = [
        partial,
        ring_sent(partial, lambda p: -1),
        ring_sent(partial, lambda p: 1),
        ring_sent(partial, lambda p: -2),
        ring_sent(partial, lambda p: 2),
        ring_sent(partial, lambda p: 3 if p % 2 else -3),
    ]
    own, other = weight_grad(place, partials, features, delta, hidden)
    back, bottom, logits_mine = spread(
        table_slot, place, zs, partials[:5], labels_mine, vectors, mine, mine_slope, dense_wide
    )
    returned = exchange_all(back)
    grad_rows = jnp.transpose(row_grad(pool_index, bag_length, returned), (0, 2, 1))

    other = shifted(other, "grp_3", 1)
    grad = (own.astype(F32) + other.astype(F32)).astype(BF16).reshape(4, 64, WIDE)
    grad = reduced_to(grad, "grp_0").reshape(4, 16, WIDE)
    for axis in ("grp_3", "grp_0"):
        bottom = summed_over(bottom, axis)
    grad, bottom = reduced_to(grad, "grp_2", bottom)
    grad, bottom = reduced_to(grad.reshape(2, 8, WIDE), "grp_1", bottom)
    grad_top = jnp.transpose(grad[:, 0:FEAT])
    grad_out = grad[:, FEAT] + grad[:, FEAT + 1]
    spots = jnp.tile(logits_mine[0:1, 0:32], (1, EMB // 32))
    row = lax.broadcasted_iota(jnp.int32, bottom.shape, 0)
    lane = lax.broadcasted_iota(jnp.int32, bottom.shape, 1)
    spare = bottom_weight.shape[0]
    bottom = jnp.where(row == spare, jnp.where(lane // 32 == me, spots, 0.0), bottom)
    bottom = summed_over(bottom, "col")
    grad_bottom = bottom[0:spare]
    logits = jnp.transpose(bottom[spare, 0:LANES].reshape(4, 2, ROWS), (1, 0, 2)).reshape(LANES)
    return (logits, grad_top, grad_out, grad_bottom, grad_rows)


def solution(mesh):
    torus = Mesh(
        mesh.devices.reshape(mesh.shape["col"], 4, 2, 4, 2),
        ("col", "grp_0", "grp_1", "grp_2", "grp_3"),
    )
    return jax.shard_map(
        step,
        mesh=torus,
        in_specs=(
            P(GRP, None, "col"),
            P(GRP, None, None),
            P(GRP, None),
            P(),
            P(GRP, None),
            P(),
            P(None, "col"),
            P("col"),
            P(GRP),
        ),
        out_specs=(P(GRP), P(None, COL_GRP), P(COL_GRP), P(), P(GRP, None, "col")),
        check_vma=False,
    )
```

```python
import jax
import jax.numpy as jnp
from jax import lax
from jax.experimental import pallas as pl
from jax.experimental.pallas import tpu as pltpu
from jax.sharding import Mesh
from jax.sharding import PartitionSpec as P


COL_GRP = ("col", "grp_0", "grp_1", "grp_2", "grp_3")
GRP = ("grp_0", "grp_1", "grp_2", "grp_3")
F32 = jnp.float32
BF16 = jnp.bfloat16

TAB = 64
ROWS = 16
LANES = 128
HALF = 64
EMB = 256
FEAT = 2336
WIDE = 2432
STEP = 8
GRAD_STEP = 16
LABEL_LANE = 36


def pieces():
    found = [(-1, 0, TAB, EMB)]
    place = EMB + TAB
    for row in range(TAB - 1):
        found.append((row, row + 1, TAB - 1 - row, place))
        place += TAB - 1 - row
    return found


def parts_of(place, count):
    found = []
    for tile in range(place // LANES, (place + count - 1) // LANES + 1):
        first = max(place, tile * LANES) - tile * LANES
        end = min(place + count, (tile + 1) * LANES) - tile * LANES
        found.append((tile, first, end))
    return found


def lane_iota(rows):
    return lax.broadcasted_iota(jnp.int32, (rows, LANES), 1)


def low_lanes(rows):
    return lane_iota(rows) < HALF


def turned(x, shift):
    shift %= LANES
    return x if shift == 0 else pltpu.roll(x, shift, 1)


def dot_t(a, b):
    return lax.dot_general(a, b, (((1,), (1,)), ((), ())), preferred_element_type=F32)


def hbm(shape, dtype):
    return pltpu.HBM(shape, dtype)


def vmem_specs(count):
    return [pl.BlockSpec(memory_space=pltpu.VMEM)] * count


def row_values():
    return lax.broadcasted_iota(jnp.int32, (256, LANES), 0).astype(F32).astype(BF16)


def counts_of(index_ref, length_ref, group, values):
    lanes = slice(group * LANES, (group + 1) * LANES)
    length = length_ref[0:1, lanes]
    one, none = jnp.ones((256, LANES), BF16), jnp.zeros((256, LANES), BF16)
    counts = none
    for slot in range(4):
        ids = jnp.where(slot < length, index_ref[0, slot : slot + 1, lanes], -1).astype(F32)
        ids = jnp.broadcast_to(ids, (16, LANES)).astype(BF16)
        counts = counts + jnp.where(jnp.concatenate([ids] * 16, axis=0) == values, one, none)
    return counts


def pool_kernel(index_ref, length_ref, rows_ref, out_ref):
    values = row_values()
    low = low_lanes(HALF)
    right = jnp.concatenate([rows_ref[0], rows_ref[0]], axis=0)
    for group in range(STEP):
        counts = counts_of(index_ref, length_ref, group, values)
        pooled = lax.dot_general(
            counts, right, (((0,), (1,)), ((), ())), preferred_element_type=F32
        )
        pooled = jnp.where(low, pooled[0:HALF], pooled[HALF:LANES]).astype(BF16)
        for peer in range(4):
            out_ref[peer, group] = pooled[peer * ROWS : (peer + 1) * ROWS]


def in_hbm(*arrays):
    return [pltpu.with_memory_space_constraint(x, pltpu.HBM) for x in arrays]


def pool(pool_index, bag_length, rows):
    return pl.pallas_call(
        pool_kernel,
        grid=(TAB // STEP,),
        in_specs=[
            pl.BlockSpec((1, 4, STEP * LANES), lambda i: (0, 0, i)),
            pl.BlockSpec((1, STEP * LANES), lambda i: (0, i)),
            pl.BlockSpec((1, HALF, 256), lambda i: (0, 0, 0)),
        ],
        out_specs=pl.BlockSpec((4, STEP, ROWS, LANES), lambda i: (0, i, 0, 0)),
        out_shape=hbm((4, TAB, ROWS, LANES), BF16),
        compiler_params=pltpu.CompilerParams(vmem_limit_bytes=12 << 20),
        name="pool",
    )(*in_hbm(pool_index, bag_length, rows))


def packed_bottom(mine_ref):
    low = low_lanes(ROWS)
    tiles = []
    for pair in range(2):
        lanes = slice(pair * LANES, (pair + 1) * LANES)
        first, second = mine_ref[0:ROWS, lanes], mine_ref[ROWS : 2 * ROWS, lanes]
        tiles.append(jnp.where(low, first, turned(second, HALF)))
        tiles.append(jnp.where(low, turned(first, HALF), second))
    return jnp.concatenate(tiles, axis=1)


def interact_kernel(slot_ref, arrived_ref, mine_ref, label_ref, out_ref, vectors_ref, spaced, gram, edge):
    def place(table, carry):
        start = pl.multiple_of(slot_ref[table] * ROWS, ROWS)
        for part in range(4):
            spaced[part, pl.ds(start, ROWS), :] = arrived_ref[part, table].astype(F32)
        return carry

    lax.fori_loop(0, TAB, place, 0, unroll=8)
    bottom = packed_bottom(mine_ref)
    low = jnp.concatenate([low_lanes(TAB)] * 4, axis=1)
    first = jnp.where(low, 1.0, 0.0).astype(BF16)
    second = jnp.where(low, 0.0, 1.0).astype(BF16)
    for row in range(ROWS):
        vectors = jnp.concatenate(
            [spaced[part, pl.ds(row, TAB, stride=ROWS), :] for part in range(4)], axis=1
        )
        narrow = vectors.astype(BF16)
        vectors_ref[row] = narrow
        right = jnp.concatenate([narrow * first, narrow * second], axis=0)
        extra = jnp.broadcast_to(bottom[row : row + 1], (ROWS, 512)).astype(BF16)
        product = dot_t(jnp.concatenate([narrow, extra], axis=0), right)
        gram[pl.ds(row, TAB, stride=ROWS), :] = product[0:TAB]
        edge[row : row + 1, :] = product[TAB : TAB + 1]

    lane = lane_iota(ROWS)
    for half in range(2):
        where = slice(half * ROWS, (half + 1) * ROWS)
        out_ref[where, 0:EMB] = mine_ref[where, :].astype(BF16)
        tile, filled = EMB // LANES, jnp.zeros((ROWS, LANES), F32)
        for row, start, count, spot in pieces():
            source = edge[...] if row < 0 else gram[row * ROWS : (row + 1) * ROWS, :]
            moved = turned(source, spot - start - half * HALF)
            for at, first, end in parts_of(spot, count):
                if at != tile:
                    out_ref[where, tile * LANES : (tile + 1) * LANES] = filled.astype(BF16)
                    tile, filled = at, jnp.zeros((ROWS, LANES), F32)
                filled = jnp.where((lane >= first) & (lane < end), moved, filled)
        filled = jnp.where(lane == LABEL_LANE, label_ref[where, :], filled)
        out_ref[where, tile * LANES : (tile + 1) * LANES] = filled.astype(BF16)


def interact(table_slot, arrived, mine, labels):
    return pl.pallas_call(
        interact_kernel,
        in_specs=[
            pl.BlockSpec(memory_space=pltpu.SMEM),
            *vmem_specs(3),
        ],
        out_specs=[pl.BlockSpec(memory_space=pltpu.VMEM)] * 2,
        out_shape=[
            jax.ShapeDtypeStruct((2 * ROWS, WIDE), BF16),
            hbm((ROWS, TAB, 512), BF16),
        ],
        scratch_shapes=[
            pltpu.VMEM((4, TAB * ROWS, LANES), F32),
            pltpu.VMEM((TAB * ROWS, LANES), F32),
            pltpu.VMEM((ROWS, LANES), F32),
        ],
        compiler_params=pltpu.CompilerParams(vmem_limit_bytes=16 << 20),
        name="interact",
    )(table_slot, arrived, mine, labels)


def top_kernel(
    f0, f1, f2, f3, weight_ref, out_weight_ref,
    all_ref, z0, z1, z2, z3, partial_ref, delta_ref, hidden_ref,
):
    for part, ref in enumerate((f0, f1, f2, f3)):
        all_ref[part * 32 : (part + 1) * 32, :] = ref[...]
    weight = weight_ref[...]
    pre = jnp.dot(all_ref[:, 0:FEAT], weight, preferred_element_type=F32)
    sigma = jax.nn.sigmoid(pre)
    hidden = (pre * sigma).astype(BF16)
    slope = sigma * (1.0 + pre * (1.0 - sigma))
    out_weight = out_weight_ref[0:1, :]
    delta = (out_weight * slope).astype(BF16)
    hidden_ref[...] = hidden
    delta_ref[...] = delta
    partial = dot_t(jnp.broadcast_to(out_weight, (16, 512)).astype(BF16), hidden)[0:8]
    for place in range(8):
        partial_ref[place] = partial
    z = dot_t(delta, weight).astype(BF16)
    for part, ref in enumerate((z0, z1, z2, z3)):
        ref[:, 0:FEAT] = z[part * 32 : (part + 1) * 32]
        ref[:, FEAT:WIDE] = jnp.zeros((32, WIDE - FEAT), BF16)


def top(parts, top_weight, out_weight):
    return pl.pallas_call(
        top_kernel,
        in_specs=vmem_specs(6),
        out_specs=vmem_specs(8),
        out_shape=[hbm((128, WIDE), BF16), hbm((32, WIDE), BF16)]
        + [jax.ShapeDtypeStruct((32, WIDE), BF16)] * 3
        + [
            jax.ShapeDtypeStruct((8, 8, LANES), F32),
            hbm((128, 512), BF16),
            hbm((128, 512), BF16),
        ],
        compiler_params=pltpu.CompilerParams(vmem_limit_bytes=24 << 20),
        name="top",
    )(*parts, top_weight, out_weight)


def own_logits(even, r0, up1, down1, up2, down2):
    return (r0 + turned(up1, -32)) + (turned(down1, -64) + turned(jnp.where(even, up2, down2), -96))


def weight_grad_kernel(
    place_ref, partial_ref, all_ref, delta_ref, hidden_ref, own_ref, other_ref, grad,
):
    even = place_ref[1] == 0
    r0, up1, down1, up2, down2, far = (partial_ref[place_ref[2 + i]] for i in range(6))

    def at(x, slot, to):
        return turned(x, 32 * (to - slot))

    own = own_logits(even, r0, up1, down1, up2, down2)
    below = at(down1, 0, 1) + r0 + at(down2, 2, 1) + at(jnp.where(even, far, up1), 3, 1)
    above = at(up1, 0, 2) + at(up2, 1, 2) + r0 + at(jnp.where(even, down1, far), 3, 2)
    across = r0 + jnp.where(
        even,
        at(down2, 0, 3) + at(down1, 1, 3) + at(far, 2, 3),
        at(up2, 0, 3) + at(far, 1, 3) + at(up1, 2, 3),
    )
    block = lane_iota(8) // 32
    logits = jnp.where(block == 0, own, jnp.where(block == 1, below, jnp.where(block == 2, above, across)))
    tile = all_ref[:, WIDE - LANES : WIDE].astype(F32)
    labels = jnp.sum(jnp.where(lane_iota(128) == LABEL_LANE, tile, 0.0), axis=1, keepdims=True)
    column = (jax.nn.sigmoid(logits.T[:, 0:1]) - labels) * (1.0 / 128.0)
    delta = (delta_ref[...].astype(F32) * column).astype(BF16)
    last = WIDE - LANES
    grad[:, 0:last] = lax.dot_general(
        delta, all_ref[:, 0:last], (((0,), (0,)), ((), ())), preferred_element_type=F32
    )
    lane = lane_iota(128)
    coarse = column.astype(BF16).astype(F32)
    spots = jnp.where(lane == 32, coarse, jnp.where(lane == 33, column - coarse, 0.0)).astype(BF16)
    grad[:, last:WIDE] = lax.dot_general(
        jnp.concatenate([delta, hidden_ref[...]], axis=0),
        jnp.concatenate([all_ref[:, last:WIDE], spots], axis=0),
        (((0,), (0,)), ((), ())),
        preferred_element_type=F32,
    )
    core = place_ref[0]
    for x in range(4):
        for y in range(4):
            for ref, which in ((own_ref, core), (other_ref, 1 - core)):
                both = []
                for z in range(2):
                    first = pl.multiple_of((((x * 2 + z) * 4 + y) * 2 + which) * 8, 8)
                    both.append(grad[pl.ds(first, 8), :])
                ref[x * 4 + y] = jnp.concatenate(both, axis=0).astype(BF16)


def weight_grad(place, partials, features, delta, hidden):
    return pl.pallas_call(
        weight_grad_kernel,
        in_specs=[pl.BlockSpec(memory_space=pltpu.SMEM)] + vmem_specs(4),
        out_specs=vmem_specs(2),
        out_shape=[
            hbm((16, 16, WIDE), BF16),
            hbm((16, 16, WIDE), BF16),
        ],
        scratch_shapes=[pltpu.VMEM((512, WIDE), F32)],
        compiler_params=pltpu.CompilerParams(vmem_limit_bytes=32 << 20),
        name="weight_grad",
    )(place, partials, *in_hbm(features, delta, hidden))


def spread_kernel(
    slot_ref, place_ref, z0, z1, z2, z3, partial_ref, label_ref, vectors_ref, mine_ref,
    slope_ref, dense_ref, back_ref, bottom_ref, logit_ref, dfeat, upper, edge, rights, dvec, dedge,
):
    logits = own_logits(place_ref[1] == 0, *(partial_ref[place_ref[2 + i]] for i in range(5)))
    logit_ref[...] = logits
    labels = jnp.sum(jnp.where(lane_iota(32) == LABEL_LANE, label_ref[...], 0.0), axis=1, keepdims=True)
    column = (jax.nn.sigmoid(logits.T[0:32, 0:1]) - labels) * (1.0 / 128.0)
    summed = z0[...].astype(F32) + z1[...].astype(F32) + z2[...].astype(F32) + z3[...].astype(F32)
    dfeat[...] = summed * column
    lane = lane_iota(ROWS)
    for row, start, count, spot in pieces():
        filled = jnp.zeros((ROWS, LANES), F32)
        for half in range(2):
            for at, first, end in parts_of(spot, count):
                source = dfeat[half * ROWS : (half + 1) * ROWS, at * LANES : (at + 1) * LANES]
                moved = turned(source, start + half * HALF - spot)
                shift = start + half * HALF - spot + at * LANES
                inside = (lane >= first + shift) & (lane < end + shift)
                filled = jnp.where(inside, moved, filled)
        filled = filled.astype(BF16).astype(F32)
        if row < 0:
            edge[...] = filled
        else:
            upper[row * ROWS : (row + 1) * ROWS, :] = filled
    upper[(TAB - 1) * ROWS :, :] = jnp.zeros((ROWS, LANES), F32)
    rights[...] = jnp.zeros_like(rights)
    bottom = packed_bottom(mine_ref)
    low = low_lanes(TAB)
    low_wide = jnp.concatenate([low] * 4, axis=1)
    low_factor = jnp.where(low_wide, 1.0, 0.0).astype(BF16)
    high_factor = jnp.where(low_wide, 0.0, 1.0).astype(BF16)
    low_few = jnp.concatenate([low_lanes(16)] * 4, axis=1)
    top_row = lax.broadcasted_iota(jnp.int32, (16, 512), 0) == 0
    for row in range(ROWS):
        half = upper[pl.ds(row, TAB, stride=ROWS), :]
        zeroth = jnp.broadcast_to(edge[row : row + 1, :], (TAB, LANES))
        flipped = jnp.concatenate([half, zeroth], axis=0).T
        first, second = flipped[0:TAB], turned(flipped[TAB : 2 * TAB], HALF)
        whole_matrix = half + jnp.where(low, first, second)
        edges = jnp.where(low, second, first)
        left = jnp.concatenate(
            [
                jnp.concatenate([whole_matrix, edges], axis=1),
                jnp.concatenate([zeroth[0:16], jnp.zeros((16, LANES), F32)], axis=1),
            ],
            axis=0,
        ).astype(BF16)
        right = rights.at[row % 2]
        right[0:TAB, :] = vectors_ref[row] * low_factor
        right[TAB : 2 * TAB, :] = vectors_ref[row] * high_factor
        own = jnp.broadcast_to(bottom[row : row + 1], (16, 512))
        right[128:144, :] = jnp.where(top_row & ~low_few, own, 0.0).astype(BF16)
        right[192:208, :] = jnp.where(top_row & low_few, own, 0.0).astype(BF16)
        product = jnp.dot(left, right[...], preferred_element_type=F32)
        for part in range(4):
            lanes = slice(part * LANES, (part + 1) * LANES)
            dvec[part, pl.ds(row, TAB, stride=ROWS), :] = product[0:TAB, lanes]
        dedge[row : row + 1, :] = product[TAB : TAB + 1]

    def place(table, carry):
        start = pl.multiple_of(slot_ref[table] * ROWS, ROWS)
        for part in range(4):
            back_ref[part, table] = dvec[part, pl.ds(start, ROWS), :].astype(BF16)
        return carry

    lax.fori_loop(0, TAB, place, 0, unroll=8)
    low = low_lanes(ROWS)
    tiles = [dedge[:, part * LANES : (part + 1) * LANES] for part in range(4)]
    own_rows = [
        jnp.concatenate(
            [jnp.where(low, tiles[2 * p], turned(tiles[2 * p + 1], HALF)) for p in range(2)], axis=1
        ),
        jnp.concatenate(
            [jnp.where(low, turned(tiles[2 * p], HALF), tiles[2 * p + 1]) for p in range(2)], axis=1
        ),
    ]
    dbottom = (dfeat[:, 0:EMB] + jnp.concatenate(own_rows, axis=0)) * slope_ref[...]
    bottom_ref[...] = lax.dot_general(
        dense_ref[...],
        dbottom,
        (((0,), (0,)), ((), ())),
        precision=lax.Precision.HIGHEST,
        preferred_element_type=F32,
    )


def spread(table_slot, place, zs, partials, labels, vectors, mine, slope, dense):
    return pl.pallas_call(
        spread_kernel,
        in_specs=[pl.BlockSpec(memory_space=pltpu.SMEM)] * 2 + vmem_specs(10),
        out_specs=vmem_specs(3),
        out_shape=[
            hbm((4, TAB, ROWS, LANES), BF16),
            jax.ShapeDtypeStruct((16, EMB), F32),
            jax.ShapeDtypeStruct((8, LANES), F32),
        ],
        scratch_shapes=[
            pltpu.VMEM((2 * ROWS, WIDE), F32),
            pltpu.VMEM((TAB * ROWS, LANES), F32),
            pltpu.VMEM((ROWS, LANES), F32),
            pltpu.VMEM((2, 256, 512), BF16),
            pltpu.VMEM((4, TAB * ROWS, LANES), F32),
            pltpu.VMEM((ROWS, 512), F32),
        ],
        compiler_params=pltpu.CompilerParams(vmem_limit_bytes=16 << 20),
        name="spread",
    )(table_slot, place, *zs, partials, labels, *in_hbm(vectors), mine, slope, dense)


def pack_kernel(place_ref, own_ref, other_ref, bottom_ref, keep_ref, s1, s2, s3, bottom_own_ref):
    high = bottom_ref[...].astype(BF16)
    low = (bottom_ref[...] - high.astype(F32)).astype(BF16)
    bottom_own_ref[...] = high.astype(F32) + low.astype(F32)
    tile = jnp.concatenate([v[:, p : p + LANES] for v in (high, low) for p in (0, LANES)], axis=0)
    for away, ref in enumerate((keep_ref, s1, s2, s3)):
        first = ((place_ref[8] + away) & 3) * 4
        for y in range(4):
            rows = slice(y * 16, (y + 1) * 16)
            total = own_ref[first + y].astype(F32) + other_ref[first + y].astype(F32)
            ref[rows, 0:WIDE] = total.astype(ref.dtype)
        if away:
            ref[:, WIDE:] = tile


def pack(place, own, other, bottom):
    return pl.pallas_call(
        pack_kernel,
        in_specs=[pl.BlockSpec(memory_space=pltpu.SMEM)] + vmem_specs(3),
        out_specs=vmem_specs(5),
        out_shape=[hbm((64, WIDE), F32)]
        + [jax.ShapeDtypeStruct((64, WIDE + LANES), BF16)] * 3
        + [jax.ShapeDtypeStruct((16, EMB), F32)],
        compiler_params=pltpu.CompilerParams(vmem_limit_bytes=16 << 20),
        name="pack",
    )(place, *in_hbm(own), other, bottom)


def count_kernel(index_ref, length_ref, out_ref):
    values = row_values()
    for group in range(STEP):
        out_ref[:, group * LANES : (group + 1) * LANES] = counts_of(index_ref, length_ref, group, values)


def count(pool_index, bag_length):
    return pl.pallas_call(
        count_kernel,
        grid=(TAB // STEP,),
        in_specs=[
            pl.BlockSpec((1, 4, STEP * LANES), lambda i: (0, 0, i)),
            pl.BlockSpec((1, STEP * LANES), lambda i: (0, i)),
        ],
        out_specs=pl.BlockSpec((256, STEP * LANES), lambda i: (0, i)),
        out_shape=hbm((256, TAB * LANES), BF16),
        compiler_params=pltpu.CompilerParams(vmem_limit_bytes=12 << 20),
        name="count",
    )(*in_hbm(pool_index, bag_length))


def row_grad_kernel(count_ref, back_ref, out_ref, total, moved):
    step = pl.program_id(0)

    @pl.when(step == 0)
    def _():
        total[...] = jnp.zeros_like(total)

    low = low_lanes(HALF)
    first = jnp.where(low, 1.0, 0.0).astype(BF16)
    second = jnp.where(low, 0.0, 1.0).astype(BF16)
    for group in range(GRAD_STEP):
        rows = jnp.concatenate([back_ref[peer, group] for peer in range(4)], axis=0)
        moved[group * LANES : group * LANES + HALF, :] = rows * first
        moved[group * LANES + HALF : (group + 1) * LANES, :] = rows * second
    total[...] += jnp.dot(count_ref[...], moved[...], preferred_element_type=F32)

    @pl.when(step == pl.num_programs(0) - 1)
    def _():
        flipped = total[...].T
        out_ref[0] = flipped[0:HALF] + flipped[HALF:LANES]


def row_grad(counts, back):
    return pl.pallas_call(
        row_grad_kernel,
        grid=(TAB // GRAD_STEP,),
        in_specs=[
            pl.BlockSpec((256, GRAD_STEP * LANES), lambda i: (0, i)),
            pl.BlockSpec((4, GRAD_STEP, ROWS, LANES), lambda i: (0, i, 0, 0)),
        ],
        out_specs=pl.BlockSpec((1, HALF, 256), lambda i: (0, 0, 0)),
        out_shape=jax.ShapeDtypeStruct((1, HALF, 256), F32),
        scratch_shapes=[
            pltpu.VMEM((256, LANES), F32),
            pltpu.VMEM((GRAD_STEP * LANES, LANES), BF16),
        ],
        compiler_params=pltpu.CompilerParams(vmem_limit_bytes=16 << 20),
        name="row_grad",
    )(*in_hbm(counts), back)


def shifted(x, axis, shift):
    size = lax.axis_size(axis)
    return lax.ppermute(x, axis, [(i, (i + shift) % size) for i in range(size)])


def ring_sent(x, moves):
    def spot(place):
        return place % 4 * 2 + place % 8 // 4

    pairs = [(spot(p), spot(p + moves(p))) for p in range(8)]
    return lax.ppermute(x, ("col", "grp_1"), pairs)


def exchange_all(x):
    flat = x.reshape(4 * TAB, ROWS, LANES)
    flat = lax.all_to_all(flat, COL_GRP, split_axis=0, concat_axis=0, tiled=True)
    return flat.reshape(4, TAB, ROWS, LANES)


def summed_over(x, axis):
    if lax.axis_size(axis) == 2:
        return x + shifted(x, axis, 1)
    others = [shifted(x, axis, shift) for shift in (1, 2, 3)]
    return (x + others[1]) + (others[0] + others[2])


def split(x):
    high = x.astype(BF16)
    return high, (x - high.astype(F32)).astype(BF16)


def reduced_to(x, axis, shared=None):
    me = lax.axis_index(axis)
    size = lax.axis_size(axis)
    total = lax.dynamic_index_in_dim(x, me, 0, keepdims=False).astype(F32)
    rows, width = total.shape
    if shared is not None:
        high, low = split(shared)
        own = high.astype(F32) + low.astype(F32)
        cuts = [v[r : r + rows] for v in (high, low) for r in range(0, shared.shape[0], rows)]
    others = []
    for shift in range(1, size):
        block = lax.dynamic_index_in_dim(x, (me + shift) % size, 0, keepdims=False).astype(BF16)
        if shared is not None:
            block = jnp.concatenate([block, *cuts], axis=1)
        block = shifted(block, axis, shift).astype(F32)
        total = total + block[:, 0:width]
        if shared is not None:
            wide = shared.shape[1]
            parts = [block[:, p : p + wide] for p in range(width, block.shape[1], wide)]
            half = len(parts) // 2
            others.append(jnp.concatenate([a + b for a, b in zip(parts[:half], parts[half:])], axis=0))
    if shared is None:
        return total
    if size == 2:
        return total, own + others[0]
    return total, (own + others[1]) + (others[0] + others[2])


def silu_slope(values):
    sigma = jax.nn.sigmoid(values)
    return sigma * (1.0 + values * (1.0 - sigma))


def step(
    table_rows,
    pool_index,
    bag_length,
    table_slot,
    dense_input,
    bottom_weight,
    top_weight,
    out_weight,
    labels,
):
    me, core = lax.axis_index("col"), lax.axis_index("grp_3")
    rows = jnp.transpose(table_rows, (0, 2, 1))
    pooled = pool(pool_index, bag_length, rows)
    arrived = exchange_all(pooled)

    dense_mine = lax.dynamic_index_in_dim(
        dense_input.reshape(2, 4, ROWS, -1), me, 1, keepdims=False
    ).reshape(2 * ROWS, -1)
    mine_pre = jnp.dot(dense_mine, bottom_weight, preferred_element_type=F32)
    mine = jax.nn.silu(mine_pre).astype(BF16).astype(F32)
    mine_slope = silu_slope(mine_pre)
    dense_wide = jnp.pad(dense_mine.astype(F32), ((0, 0), (0, 16 - dense_mine.shape[1])))
    labels_mine = lax.dynamic_index_in_dim(labels.reshape(2, 4, ROWS), me, 1, keepdims=False)
    labels_mine = jnp.broadcast_to(labels_mine.astype(F32).reshape(2 * ROWS, 1), (2 * ROWS, LANES))
    spot = lax.axis_index("grp_1") * 4 + me
    near = [spot, spot + 1, spot - 1, spot + 2, spot - 2, jnp.where(me % 2 == 0, spot - 3, spot + 3)]
    near = [p % 4 * 2 + p % 8 // 4 for p in near]
    place = jnp.stack([core, me % 2, *near, lax.axis_index("grp_0")]).astype(jnp.int32)
    out_weight_row = out_weight.astype(F32).reshape(1, -1)

    counts = count(pool_index, bag_length)
    part, vectors = interact(table_slot, arrived, mine, labels_mine)
    parts = [
        part,
        ring_sent(part, lambda p: 1),
        ring_sent(part, lambda p: -1),
        ring_sent(part, lambda p: -2 if p % 2 else 2),
    ]
    features, *zs, partial, delta, hidden = top(parts, top_weight, out_weight_row)
    zs = [
        zs[0],
        ring_sent(zs[1], lambda p: -1),
        ring_sent(zs[2], lambda p: 1),
        ring_sent(zs[3], lambda p: 2 if p % 2 else -2),
    ]
    partials = lax.all_to_all(partial, ("col", "grp_1"), split_axis=0, concat_axis=0, tiled=True)
    own, other = weight_grad(place, partials, features, delta, hidden)
    back, bottom, logits_mine = spread(
        table_slot, place, zs, partials, labels_mine, vectors, mine, mine_slope, dense_wide
    )
    returned = exchange_all(back)
    grad_rows = jnp.transpose(row_grad(counts, returned), (0, 2, 1))

    other = shifted(other, "grp_3", 1)
    grad, *blocks, bottom = pack(place, own, other, bottom)
    sums = []
    for away in (1, 2, 3):
        block = shifted(blocks[away - 1], "grp_0", away).astype(F32)
        grad = grad + block[:, 0:WIDE]
        tile = block[0:32, WIDE:] + block[32:64, WIDE:]
        sums.append(jnp.concatenate([tile[0:16], tile[16:32]], axis=1))
    grad = grad.reshape(4, 16, WIDE)
    bottom = summed_over((bottom + sums[1]) + (sums[0] + sums[2]), "grp_3")
    grad, bottom = reduced_to(grad, "grp_2", bottom)
    grad, bottom = reduced_to(grad.reshape(2, 8, WIDE), "grp_1", bottom)
    grad_top = jnp.transpose(grad[:, 0:FEAT])
    grad_out = grad[:, FEAT] + grad[:, FEAT + 1]
    spots = jnp.tile(logits_mine[0:1, 0:32], (1, EMB // 32))
    row = lax.broadcasted_iota(jnp.int32, bottom.shape, 0)
    lane = lax.broadcasted_iota(jnp.int32, bottom.shape, 1)
    spare = bottom_weight.shape[0]
    bottom = jnp.where(row == spare, jnp.where(lane // 32 == me, spots, 0.0), bottom)
    bottom = summed_over(bottom, "col")
    grad_bottom = bottom[0:spare]
    logits = jnp.transpose(bottom[spare, 0:LANES].reshape(4, 2, ROWS), (1, 0, 2)).reshape(LANES)
    return (logits, grad_top, grad_out, grad_bottom, grad_rows)


def solution(mesh):
    torus = Mesh(
        mesh.devices.reshape(mesh.shape["col"], 4, 2, 4, 2),
        ("col", "grp_0", "grp_1", "grp_2", "grp_3"),
    )
    return jax.shard_map(
        step,
        mesh=torus,
        in_specs=(
            P(GRP, None, "col"),
            P(GRP, None, None),
            P(GRP, None),
            P(),
            P(GRP, None),
            P(),
            P(None, "col"),
            P("col"),
            P(GRP),
        ),
        out_specs=(P(GRP), P(None, COL_GRP), P(COL_GRP), P(), P(GRP, None, "col")),
        check_vma=False,
    )
```

```python
import jax
import jax.numpy as jnp
from jax import lax
from jax.experimental import pallas as pl
from jax.experimental.pallas import tpu as pltpu
from jax.sharding import Mesh
from jax.sharding import PartitionSpec as P


COL_GRP = ("col", "grp_0", "grp_1", "grp_2", "grp_3")
GRP = ("grp_0", "grp_1", "grp_2", "grp_3")
F32 = jnp.float32
BF16 = jnp.bfloat16

TAB = 64
ROWS = 16
APART = 24
LANES = 128
HALF = 64
EMB = 256
FEAT = 2336
WIDE = 2432
STEP = 16
GRAD_STEP = 16
LABEL_LANE = 36


def pieces():
    found = [(-1, 0, TAB, EMB)]
    place = EMB + TAB
    for row in range(TAB - 1):
        found.append((row, row + 1, TAB - 1 - row, place))
        place += TAB - 1 - row
    return found


def parts_of(place, count):
    found = []
    for tile in range(place // LANES, (place + count - 1) // LANES + 1):
        first = max(place, tile * LANES) - tile * LANES
        end = min(place + count, (tile + 1) * LANES) - tile * LANES
        found.append((tile, first, end))
    return found


def lane_iota(rows):
    return lax.broadcasted_iota(jnp.int32, (rows, LANES), 1)


def low_lanes(rows):
    return lane_iota(rows) < HALF


def turned(x, shift):
    shift %= LANES
    return x if shift == 0 else pltpu.roll(x, shift, 1)


def dot_t(a, b):
    return lax.dot_general(a, b, (((1,), (1,)), ((), ())), preferred_element_type=F32)


def hbm(shape, dtype):
    return pltpu.HBM(shape, dtype)


def vmem_specs(count):
    return [pl.BlockSpec(memory_space=pltpu.VMEM)] * count


def row_values():
    return lax.broadcasted_iota(jnp.int32, (256, LANES), 0).astype(F32).astype(BF16)


def counts_of(index_ref, length_ref, group, values):
    lanes = slice(group * LANES, (group + 1) * LANES)
    length = length_ref[0:1, lanes]
    one, none = jnp.ones((256, LANES), BF16), jnp.zeros((256, LANES), BF16)
    counts = none
    for slot in range(4):
        ids = jnp.where(slot < length, index_ref[0, slot : slot + 1, lanes], -1).astype(F32)
        ids = jnp.broadcast_to(ids, (16, LANES)).astype(BF16)
        counts = counts + jnp.where(jnp.concatenate([ids] * 16, axis=0) == values, one, none)
    return counts


def pool_kernel(index_ref, length_ref, rows_ref, out_ref):
    values = row_values()
    low = low_lanes(HALF)
    right = jnp.concatenate([rows_ref[0], rows_ref[0]], axis=0)
    for group in range(STEP):
        counts = counts_of(index_ref, length_ref, group, values)
        pooled = lax.dot_general(
            counts, right, (((0,), (1,)), ((), ())), preferred_element_type=F32
        )
        pooled = jnp.where(low, pooled[0:HALF], pooled[HALF:LANES]).astype(BF16)
        for peer in range(4):
            out_ref[peer, group] = pooled[peer * ROWS : (peer + 1) * ROWS]


def in_hbm(*arrays):
    return [pltpu.with_memory_space_constraint(x, pltpu.HBM) for x in arrays]


def pool(pool_index, bag_length, rows):
    return pl.pallas_call(
        pool_kernel,
        grid=(TAB // STEP,),
        in_specs=[
            pl.BlockSpec((1, 4, STEP * LANES), lambda i: (0, 0, i)),
            pl.BlockSpec((1, STEP * LANES), lambda i: (0, i)),
            pl.BlockSpec((1, HALF, 256), lambda i: (0, 0, 0)),
        ],
        out_specs=pl.BlockSpec((4, STEP, ROWS, LANES), lambda i: (0, i, 0, 0)),
        out_shape=hbm((4, TAB, ROWS, LANES), BF16),
        compiler_params=pltpu.CompilerParams(vmem_limit_bytes=12 << 20),
        name="pool",
    )(*in_hbm(pool_index, bag_length, rows))


def packed_bottom(mine_ref):
    low = low_lanes(ROWS)
    tiles = []
    for pair in range(2):
        lanes = slice(pair * LANES, (pair + 1) * LANES)
        first, second = mine_ref[0:ROWS, lanes], mine_ref[ROWS : 2 * ROWS, lanes]
        tiles.append(jnp.where(low, first, turned(second, HALF)))
        tiles.append(jnp.where(low, turned(first, HALF), second))
    return jnp.concatenate(tiles, axis=1)


def interact_kernel(slot_ref, arrived_ref, mine_ref, label_ref, out_ref, vectors_ref, spaced, gram, edge):
    def place(table, carry):
        start = pl.multiple_of(slot_ref[table] * APART, 8)
        for part in range(4):
            spaced[part, pl.ds(start, ROWS), :] = arrived_ref[part, table].astype(F32)
        return carry

    lax.fori_loop(0, TAB, place, 0, unroll=8)
    bottom = packed_bottom(mine_ref)
    low = jnp.concatenate([low_lanes(TAB)] * 4, axis=1)
    first = jnp.where(low, 1.0, 0.0).astype(BF16)
    second = jnp.where(low, 0.0, 1.0).astype(BF16)
    for row in range(ROWS):
        vectors = jnp.concatenate(
            [spaced[part, pl.ds(row, TAB, stride=APART), :] for part in range(4)], axis=1
        )
        narrow = vectors.astype(BF16)
        vectors_ref[row] = narrow
        right = jnp.concatenate([narrow * first, narrow * second], axis=0)
        extra = jnp.broadcast_to(bottom[row : row + 1], (ROWS, 512)).astype(BF16)
        product = dot_t(jnp.concatenate([narrow, extra], axis=0), right)
        gram[pl.ds(row, TAB, stride=APART), :] = product[0:TAB]
        edge[row : row + 1, :] = product[TAB : TAB + 1]

    lane = lane_iota(ROWS)
    for half in range(2):
        where = slice(half * ROWS, (half + 1) * ROWS)
        out_ref[where, 0:EMB] = mine_ref[where, :].astype(BF16)
        tile, filled = EMB // LANES, jnp.zeros((ROWS, LANES), F32)
        for row, start, count, spot in pieces():
            source = edge[...] if row < 0 else gram[row * APART : row * APART + ROWS, :]
            moved = turned(source, spot - start - half * HALF)
            for at, first, _ in parts_of(spot, count):
                if at != tile:
                    out_ref[where, tile * LANES : (tile + 1) * LANES] = filled.astype(BF16)
                    tile, filled = at, moved
                filled = moved if first == 0 else jnp.where(lane >= first, moved, filled)
        filled = jnp.where(lane < FEAT % LANES, filled, jnp.where(lane == LABEL_LANE, label_ref[where, :], 0.0))
        out_ref[where, tile * LANES : (tile + 1) * LANES] = filled.astype(BF16)


def interact(table_slot, arrived, mine, labels):
    return pl.pallas_call(
        interact_kernel,
        in_specs=[
            pl.BlockSpec(memory_space=pltpu.SMEM),
            *vmem_specs(3),
        ],
        out_specs=[pl.BlockSpec(memory_space=pltpu.VMEM)] * 2,
        out_shape=[
            jax.ShapeDtypeStruct((2 * ROWS, WIDE), BF16),
            hbm((ROWS, TAB, 512), BF16),
        ],
        scratch_shapes=[
            pltpu.VMEM((4, TAB * APART, LANES), F32),
            pltpu.VMEM((TAB * APART, LANES), F32),
            pltpu.VMEM((ROWS, LANES), F32),
        ],
        compiler_params=pltpu.CompilerParams(vmem_limit_bytes=16 << 20),
        name="interact",
    )(table_slot, arrived, mine, labels)


def top_kernel(
    f0, f1, f2, f3, weight_ref, out_weight_ref,
    all_ref, z0, z1, z2, z3, partial_ref, delta_ref, hidden_ref,
):
    for part, ref in enumerate((f0, f1, f2, f3)):
        all_ref[part * 32 : (part + 1) * 32, :] = ref[...]
    weight = weight_ref[...]
    pre = jnp.dot(all_ref[:, 0:FEAT], weight, preferred_element_type=F32)
    sigma = jax.nn.sigmoid(pre)
    hidden = (pre * sigma).astype(BF16)
    slope = sigma * (1.0 + pre * (1.0 - sigma))
    out_weight = out_weight_ref[0:1, :]
    delta = (out_weight * slope).astype(BF16)
    hidden_ref[...] = hidden
    delta_ref[...] = delta
    partial = dot_t(jnp.broadcast_to(out_weight, (16, 512)).astype(BF16), hidden)[0:8]
    for place in range(8):
        partial_ref[place] = partial
    z = dot_t(delta, weight).astype(BF16)
    for part, ref in enumerate((z0, z1, z2, z3)):
        ref[:, 0:FEAT] = z[part * 32 : (part + 1) * 32]
        ref[:, FEAT:WIDE] = jnp.zeros((32, WIDE - FEAT), BF16)


def top(parts, top_weight, out_weight):
    return pl.pallas_call(
        top_kernel,
        in_specs=vmem_specs(6),
        out_specs=vmem_specs(8),
        out_shape=[hbm((128, WIDE), BF16), hbm((32, WIDE), BF16)]
        + [jax.ShapeDtypeStruct((32, WIDE), BF16)] * 3
        + [
            jax.ShapeDtypeStruct((8, 8, LANES), F32),
            hbm((128, 512), BF16),
            hbm((128, 512), BF16),
        ],
        compiler_params=pltpu.CompilerParams(vmem_limit_bytes=24 << 20),
        name="top",
    )(*parts, top_weight, out_weight)


def own_logits(even, r0, up1, down1, up2, down2):
    return (r0 + turned(up1, -32)) + (turned(down1, -64) + turned(jnp.where(even, up2, down2), -96))


def weight_grad_kernel(
    place_ref, partial_ref, all_ref, delta_ref, hidden_ref, own_ref, other_ref, grad,
):
    even = place_ref[1] == 0
    r0, up1, down1, up2, down2, far = (partial_ref[place_ref[2 + i]] for i in range(6))

    def at(x, slot, to):
        return turned(x, 32 * (to - slot))

    own = own_logits(even, r0, up1, down1, up2, down2)
    below = at(down1, 0, 1) + r0 + at(down2, 2, 1) + at(jnp.where(even, far, up1), 3, 1)
    above = at(up1, 0, 2) + at(up2, 1, 2) + r0 + at(jnp.where(even, down1, far), 3, 2)
    across = r0 + jnp.where(
        even,
        at(down2, 0, 3) + at(down1, 1, 3) + at(far, 2, 3),
        at(up2, 0, 3) + at(far, 1, 3) + at(up1, 2, 3),
    )
    block = lane_iota(8) // 32
    logits = jnp.where(block == 0, own, jnp.where(block == 1, below, jnp.where(block == 2, above, across)))
    tile = all_ref[:, WIDE - LANES : WIDE].astype(F32)
    labels = jnp.sum(jnp.where(lane_iota(128) == LABEL_LANE, tile, 0.0), axis=1, keepdims=True)
    column = (jax.nn.sigmoid(logits.T[:, 0:1]) - labels) * (1.0 / 128.0)
    delta = (delta_ref[...].astype(F32) * column).astype(BF16)
    last = WIDE - LANES
    grad[:, 0:last] = lax.dot_general(
        delta, all_ref[:, 0:last], (((0,), (0,)), ((), ())), preferred_element_type=F32
    )
    lane = lane_iota(128)
    coarse = column.astype(BF16).astype(F32)
    spots = jnp.where(lane == 32, coarse, jnp.where(lane == 33, column - coarse, 0.0)).astype(BF16)
    grad[:, last:WIDE] = lax.dot_general(
        jnp.concatenate([delta, hidden_ref[...]], axis=0),
        jnp.concatenate([all_ref[:, last:WIDE], spots], axis=0),
        (((0,), (0,)), ((), ())),
        preferred_element_type=F32,
    )
    core = place_ref[0]
    for x in range(4):
        for y in range(4):
            for ref, which in ((own_ref, core), (other_ref, 1 - core)):
                both = []
                for z in range(2):
                    first = pl.multiple_of((((x * 2 + z) * 4 + y) * 2 + which) * 8, 8)
                    both.append(grad[pl.ds(first, 8), :])
                ref[x * 4 + y] = jnp.concatenate(both, axis=0).astype(BF16)


def weight_grad(place, partials, features, delta, hidden):
    return pl.pallas_call(
        weight_grad_kernel,
        in_specs=[pl.BlockSpec(memory_space=pltpu.SMEM)] + vmem_specs(4),
        out_specs=vmem_specs(2),
        out_shape=[
            hbm((16, 16, WIDE), BF16),
            hbm((16, 16, WIDE), BF16),
        ],
        scratch_shapes=[pltpu.VMEM((512, WIDE), F32)],
        compiler_params=pltpu.CompilerParams(vmem_limit_bytes=32 << 20),
        name="weight_grad",
    )(place, partials, *in_hbm(features, delta, hidden))


def spread_kernel(
    slot_ref, place_ref, z0, z1, z2, z3, partial_ref, label_ref, vectors_ref, mine_ref,
    slope_ref, dense_ref, back_ref, bottom_ref, logit_ref, dfeat, dpairs, upper, edge, dvec, dedge,
):
    logits = own_logits(place_ref[1] == 0, *(partial_ref[place_ref[2 + i]] for i in range(5)))
    logit_ref[...] = logits
    labels = jnp.sum(jnp.where(lane_iota(32) == LABEL_LANE, label_ref[...], 0.0), axis=1, keepdims=True)
    column = (jax.nn.sigmoid(logits.T[0:32, 0:1]) - labels) * (1.0 / 128.0)
    summed = z0[...].astype(F32) + z1[...].astype(F32) + z2[...].astype(F32) + z3[...].astype(F32)
    summed = summed * column
    dfeat[...] = summed[:, 0:EMB]
    dpairs[...] = summed.astype(BF16).astype(F32)
    lane = lane_iota(ROWS)
    none = jnp.zeros((ROWS, LANES), F32)
    for row, start, count, spot in pieces():
        filled = none
        for half in range(2):
            for at, first, _ in parts_of(spot, count):
                source = dpairs[half * ROWS : (half + 1) * ROWS, at * LANES : (at + 1) * LANES]
                moved = turned(source, start + half * HALF - spot)
                begin = first + start + half * HALF - spot + at * LANES
                filled = jnp.where(lane >= begin, moved, filled)
            if half == 0 and row >= 0:
                filled = jnp.where(lane >= HALF, 0.0, filled)
        if row < 0:
            edge[...] = filled
        else:
            upper[row * APART : row * APART + ROWS, :] = filled
    upper[(TAB - 1) * APART : (TAB - 1) * APART + ROWS, :] = jnp.zeros((ROWS, LANES), F32)
    bottom = packed_bottom(mine_ref)
    low = low_lanes(TAB)
    low_wide = jnp.concatenate([low] * 4, axis=1)
    low_factor = jnp.where(low_wide, 1.0, 0.0).astype(BF16)
    high_factor = jnp.where(low_wide, 0.0, 1.0).astype(BF16)
    low_few = jnp.concatenate([low_lanes(16)] * 4, axis=1)
    top_row = lax.broadcasted_iota(jnp.int32, (16, 512), 0) == 0
    low_own = jnp.where(top_row & low_few, 1.0, 0.0).astype(BF16)
    high_own = jnp.where(top_row & ~low_few, 1.0, 0.0).astype(BF16)
    empty = jnp.zeros((48, 512), BF16)
    for row in range(ROWS):
        half = upper[pl.ds(row, TAB, stride=APART), :]
        zeroth = jnp.broadcast_to(edge[row : row + 1, :], (TAB, LANES))
        flipped = jnp.concatenate([half, zeroth], axis=0).T
        first, second = flipped[0:TAB], turned(flipped[TAB : 2 * TAB], HALF)
        whole_matrix = half + jnp.where(low, first, second)
        edges = jnp.where(low, second, first)
        left = jnp.concatenate(
            [
                jnp.concatenate([whole_matrix, edges], axis=1),
                jnp.concatenate([zeroth[0:16], jnp.zeros((16, LANES), F32)], axis=1),
            ],
            axis=0,
        ).astype(BF16)
        vectors = vectors_ref[row]
        own = jnp.broadcast_to(bottom[row : row + 1], (16, 512)).astype(BF16)
        right = jnp.concatenate(
            [vectors * low_factor, vectors * high_factor, own * high_own, empty, own * low_own, empty], axis=0
        )
        product = jnp.dot(left, right, preferred_element_type=F32)
        for part in range(4):
            lanes = slice(part * LANES, (part + 1) * LANES)
            dvec[part, pl.ds(row, TAB, stride=APART), :] = product[0:TAB, lanes]
        dedge[row : row + 1, :] = product[TAB : TAB + 1]

    def place(table, carry):
        start = pl.multiple_of(slot_ref[table] * APART, 8)
        for part in range(4):
            back_ref[part, table] = dvec[part, pl.ds(start, ROWS), :].astype(BF16)
        return carry

    lax.fori_loop(0, TAB, place, 0, unroll=8)
    low = low_lanes(ROWS)
    tiles = [dedge[:, part * LANES : (part + 1) * LANES] for part in range(4)]
    own_rows = [
        jnp.concatenate(
            [jnp.where(low, tiles[2 * p], turned(tiles[2 * p + 1], HALF)) for p in range(2)], axis=1
        ),
        jnp.concatenate(
            [jnp.where(low, turned(tiles[2 * p], HALF), tiles[2 * p + 1]) for p in range(2)], axis=1
        ),
    ]
    dbottom = (dfeat[...] + jnp.concatenate(own_rows, axis=0)) * slope_ref[...]
    bottom_ref[...] = lax.dot_general(
        dense_ref[...],
        dbottom,
        (((0,), (0,)), ((), ())),
        precision=lax.Precision.HIGHEST,
        preferred_element_type=F32,
    )


def spread(table_slot, place, zs, partials, labels, vectors, mine, slope, dense):
    return pl.pallas_call(
        spread_kernel,
        in_specs=[pl.BlockSpec(memory_space=pltpu.SMEM)] * 2 + vmem_specs(10),
        out_specs=vmem_specs(3),
        out_shape=[
            hbm((4, TAB, ROWS, LANES), BF16),
            jax.ShapeDtypeStruct((16, EMB), F32),
            jax.ShapeDtypeStruct((8, LANES), F32),
        ],
        scratch_shapes=[
            pltpu.VMEM((2 * ROWS, EMB), F32),
            pltpu.VMEM((2 * ROWS, WIDE), F32),
            pltpu.VMEM((TAB * APART, LANES), F32),
            pltpu.VMEM((ROWS, LANES), F32),
            pltpu.VMEM((4, TAB * APART, LANES), F32),
            pltpu.VMEM((ROWS, 512), F32),
        ],
        compiler_params=pltpu.CompilerParams(vmem_limit_bytes=16 << 20),
        name="spread",
    )(table_slot, place, *zs, partials, labels, *in_hbm(vectors), mine, slope, dense)


def pack_kernel(place_ref, own_ref, other_ref, bottom_ref, keep_ref, s1, s2, s3, bottom_own_ref):
    high = bottom_ref[...].astype(BF16)
    low = (bottom_ref[...] - high.astype(F32)).astype(BF16)
    bottom_own_ref[...] = high.astype(F32) + low.astype(F32)
    tile = jnp.concatenate([v[:, p : p + LANES] for v in (high, low) for p in (0, LANES)], axis=0)
    for away, ref in enumerate((keep_ref, s1, s2, s3)):
        first = ((place_ref[8] + away) & 3) * 4
        for y in range(4):
            rows = slice(y * 16, (y + 1) * 16)
            total = own_ref[first + y].astype(F32) + other_ref[first + y].astype(F32)
            ref[rows, 0:WIDE] = total.astype(ref.dtype)
        if away:
            ref[:, WIDE:] = tile


def pack(place, own, other, bottom):
    return pl.pallas_call(
        pack_kernel,
        in_specs=[pl.BlockSpec(memory_space=pltpu.SMEM)] + vmem_specs(3),
        out_specs=vmem_specs(5),
        out_shape=[hbm((64, WIDE), F32)]
        + [jax.ShapeDtypeStruct((64, WIDE + LANES), BF16)] * 3
        + [jax.ShapeDtypeStruct((16, EMB), F32)],
        compiler_params=pltpu.CompilerParams(vmem_limit_bytes=16 << 20),
        name="pack",
    )(place, *in_hbm(own), other, bottom)


def count_kernel(index_ref, length_ref, out_ref):
    values = row_values()
    for group in range(STEP):
        out_ref[:, group * LANES : (group + 1) * LANES] = counts_of(index_ref, length_ref, group, values)


def count(pool_index, bag_length):
    return pl.pallas_call(
        count_kernel,
        grid=(TAB // STEP,),
        in_specs=[
            pl.BlockSpec((1, 4, STEP * LANES), lambda i: (0, 0, i)),
            pl.BlockSpec((1, STEP * LANES), lambda i: (0, i)),
        ],
        out_specs=pl.BlockSpec((256, STEP * LANES), lambda i: (0, i)),
        out_shape=hbm((256, TAB * LANES), BF16),
        compiler_params=pltpu.CompilerParams(vmem_limit_bytes=12 << 20),
        name="count",
    )(*in_hbm(pool_index, bag_length))


def row_grad_kernel(count_ref, back_ref, out_ref, total, moved):
    step = pl.program_id(0)

    @pl.when(step == 0)
    def _():
        total[...] = jnp.zeros_like(total)

    low = low_lanes(HALF)
    first = jnp.where(low, 1.0, 0.0).astype(BF16)
    second = jnp.where(low, 0.0, 1.0).astype(BF16)
    for group in range(GRAD_STEP):
        rows = jnp.concatenate([back_ref[peer, group] for peer in range(4)], axis=0)
        moved[group * LANES : group * LANES + HALF, :] = rows * first
        moved[group * LANES + HALF : (group + 1) * LANES, :] = rows * second
    total[...] += jnp.dot(count_ref[...], moved[...], preferred_element_type=F32)

    @pl.when(step == pl.num_programs(0) - 1)
    def _():
        flipped = total[...].T
        out_ref[0] = flipped[0:HALF] + flipped[HALF:LANES]


def row_grad(counts, back):
    return pl.pallas_call(
        row_grad_kernel,
        grid=(TAB // GRAD_STEP,),
        in_specs=[
            pl.BlockSpec((256, GRAD_STEP * LANES), lambda i: (0, i)),
            pl.BlockSpec((4, GRAD_STEP, ROWS, LANES), lambda i: (0, i, 0, 0)),
        ],
        out_specs=pl.BlockSpec((1, HALF, 256), lambda i: (0, 0, 0)),
        out_shape=jax.ShapeDtypeStruct((1, HALF, 256), F32),
        scratch_shapes=[
            pltpu.VMEM((256, LANES), F32),
            pltpu.VMEM((GRAD_STEP * LANES, LANES), BF16),
        ],
        compiler_params=pltpu.CompilerParams(vmem_limit_bytes=16 << 20),
        name="row_grad",
    )(*in_hbm(counts), back)


def shifted(x, axis, shift):
    size = lax.axis_size(axis)
    return lax.ppermute(x, axis, [(i, (i + shift) % size) for i in range(size)])


def ring_sent(x, moves):
    def spot(place):
        return place % 4 * 2 + place % 8 // 4

    pairs = [(spot(p), spot(p + moves(p))) for p in range(8)]
    return lax.ppermute(x, ("col", "grp_1"), pairs)


def exchange_all(x):
    flat = x.reshape(4 * TAB, ROWS, LANES)
    flat = lax.all_to_all(flat, COL_GRP, split_axis=0, concat_axis=0, tiled=True)
    return flat.reshape(4, TAB, ROWS, LANES)


def summed_over(x, axis):
    if lax.axis_size(axis) == 2:
        return x + shifted(x, axis, 1)
    others = [shifted(x, axis, shift) for shift in (1, 2, 3)]
    return (x + others[1]) + (others[0] + others[2])


def split(x):
    high = x.astype(BF16)
    return high, (x - high.astype(F32)).astype(BF16)


def reduced_to(x, axis, shared=None):
    me = lax.axis_index(axis)
    size = lax.axis_size(axis)
    total = lax.dynamic_index_in_dim(x, me, 0, keepdims=False).astype(F32)
    rows, width = total.shape
    if shared is not None:
        high, low = split(shared)
        own = high.astype(F32) + low.astype(F32)
        cuts = [v[r : r + rows] for v in (high, low) for r in range(0, shared.shape[0], rows)]
    others = []
    for shift in range(1, size):
        block = lax.dynamic_index_in_dim(x, (me + shift) % size, 0, keepdims=False).astype(BF16)
        if shared is not None:
            block = jnp.concatenate([block, *cuts], axis=1)
        block = shifted(block, axis, shift).astype(F32)
        total = total + block[:, 0:width]
        if shared is not None:
            wide = shared.shape[1]
            parts = [block[:, p : p + wide] for p in range(width, block.shape[1], wide)]
            half = len(parts) // 2
            others.append(jnp.concatenate([a + b for a, b in zip(parts[:half], parts[half:])], axis=0))
    if shared is None:
        return total
    if size == 2:
        return total, own + others[0]
    return total, (own + others[1]) + (others[0] + others[2])


def silu_slope(values):
    sigma = jax.nn.sigmoid(values)
    return sigma * (1.0 + values * (1.0 - sigma))


def step(
    table_rows,
    pool_index,
    bag_length,
    table_slot,
    dense_input,
    bottom_weight,
    top_weight,
    out_weight,
    labels,
):
    me, core = lax.axis_index("col"), lax.axis_index("grp_3")
    rows = jnp.transpose(table_rows, (0, 2, 1))
    pooled = pool(pool_index, bag_length, rows)
    arrived = exchange_all(pooled)

    dense_mine = lax.dynamic_index_in_dim(
        dense_input.reshape(2, 4, ROWS, -1), me, 1, keepdims=False
    ).reshape(2 * ROWS, -1)
    mine_pre = jnp.dot(dense_mine, bottom_weight, preferred_element_type=F32)
    mine = jax.nn.silu(mine_pre).astype(BF16).astype(F32)
    mine_slope = silu_slope(mine_pre)
    dense_wide = jnp.pad(dense_mine.astype(F32), ((0, 0), (0, 16 - dense_mine.shape[1])))
    labels_mine = lax.dynamic_index_in_dim(labels.reshape(2, 4, ROWS), me, 1, keepdims=False)
    labels_mine = jnp.broadcast_to(labels_mine.astype(F32).reshape(2 * ROWS, 1), (2 * ROWS, LANES))
    spot = lax.axis_index("grp_1") * 4 + me
    near = [spot, spot + 1, spot - 1, spot + 2, spot - 2, jnp.where(me % 2 == 0, spot - 3, spot + 3)]
    near = [p % 4 * 2 + p % 8 // 4 for p in near]
    place = jnp.stack([core, me % 2, *near, lax.axis_index("grp_0")]).astype(jnp.int32)
    out_weight_row = out_weight.astype(F32).reshape(1, -1)

    counts = count(pool_index, bag_length)
    part, vectors = interact(table_slot, arrived, mine, labels_mine)
    parts = [
        part,
        ring_sent(part, lambda p: 1),
        ring_sent(part, lambda p: -1),
        ring_sent(part, lambda p: -2 if p % 2 else 2),
    ]
    features, *zs, partial, delta, hidden = top(parts, top_weight, out_weight_row)
    zs = [
        zs[0],
        ring_sent(zs[1], lambda p: -1),
        ring_sent(zs[2], lambda p: 1),
        ring_sent(zs[3], lambda p: 2 if p % 2 else -2),
    ]
    partials = lax.all_to_all(partial, ("col", "grp_1"), split_axis=0, concat_axis=0, tiled=True)
    own, other = weight_grad(place, partials, features, delta, hidden)
    back, bottom, logits_mine = spread(
        table_slot, place, zs, partials, labels_mine, vectors, mine, mine_slope, dense_wide
    )
    returned = exchange_all(back)
    grad_rows = jnp.transpose(row_grad(counts, returned), (0, 2, 1))

    other = shifted(other, "grp_3", 1)
    grad, *blocks, bottom = pack(place, own, other, bottom)
    sums = []
    for away in (1, 2, 3):
        block = shifted(blocks[away - 1], "grp_0", away).astype(F32)
        grad = grad + block[:, 0:WIDE]
        tile = block[0:32, WIDE:] + block[32:64, WIDE:]
        sums.append(jnp.concatenate([tile[0:16], tile[16:32]], axis=1))
    grad = grad.reshape(4, 16, WIDE)
    bottom = summed_over((bottom + sums[1]) + (sums[0] + sums[2]), "grp_3")
    grad, bottom = reduced_to(grad, "grp_2", bottom)
    grad, bottom = reduced_to(grad.reshape(2, 8, WIDE), "grp_1", bottom)
    grad_top = jnp.transpose(grad[:, 0:FEAT])
    grad_out = grad[:, FEAT] + grad[:, FEAT + 1]
    spots = jnp.tile(logits_mine[0:1, 0:32], (1, EMB // 32))
    row = lax.broadcasted_iota(jnp.int32, bottom.shape, 0)
    lane = lax.broadcasted_iota(jnp.int32, bottom.shape, 1)
    spare = bottom_weight.shape[0]
    bottom = jnp.where(row == spare, jnp.where(lane // 32 == me, spots, 0.0), bottom)
    bottom = summed_over(bottom, "col")
    grad_bottom = bottom[0:spare]
    logits = jnp.transpose(bottom[spare, 0:LANES].reshape(4, 2, ROWS), (1, 0, 2)).reshape(LANES)
    return (logits, grad_top, grad_out, grad_bottom, grad_rows)


def solution(mesh):
    torus = Mesh(
        mesh.devices.reshape(mesh.shape["col"], 4, 2, 4, 2),
        ("col", "grp_0", "grp_1", "grp_2", "grp_3"),
    )
    return jax.shard_map(
        step,
        mesh=torus,
        in_specs=(
            P(GRP, None, "col"),
            P(GRP, None, None),
            P(GRP, None),
            P(),
            P(GRP, None),
            P(),
            P(None, "col"),
            P("col"),
            P(GRP),
        ),
        out_specs=(P(GRP), P(None, COL_GRP), P(COL_GRP), P(), P(GRP, None, "col")),
        check_vma=False,
    )
```

```python
import jax
import jax.numpy as jnp
from jax import lax
from jax.experimental import pallas as pl
from jax.experimental.pallas import tpu as pltpu
from jax.sharding import Mesh
from jax.sharding import PartitionSpec as P


COL_GRP = ("col", "grp_0", "grp_1", "grp_2", "grp_3")
GRP = ("grp_0", "grp_1", "grp_2", "grp_3")
F32 = jnp.float32
BF16 = jnp.bfloat16

TAB = 64
ROWS = 16
APART = 24
LANES = 128
HALF = 64
EMB = 256
FEAT = 2336
WIDE = 2432
STEP = 32
GRAD_STEP = 16
LABEL_LANE = 36


def pieces():
    found = [(-1, 0, TAB, EMB)]
    place = EMB + TAB
    for row in range(TAB - 1):
        found.append((row, row + 1, TAB - 1 - row, place))
        place += TAB - 1 - row
    return found


def parts_of(place, count):
    found = []
    for tile in range(place // LANES, (place + count - 1) // LANES + 1):
        first = max(place, tile * LANES) - tile * LANES
        end = min(place + count, (tile + 1) * LANES) - tile * LANES
        found.append((tile, first, end))
    return found


def lane_iota(rows):
    return lax.broadcasted_iota(jnp.int32, (rows, LANES), 1)


def low_lanes(rows):
    return lane_iota(rows) < HALF


def turned(x, shift):
    shift %= LANES
    return x if shift == 0 else pltpu.roll(x, shift, 1)


def dot_t(a, b):
    return lax.dot_general(a, b, (((1,), (1,)), ((), ())), preferred_element_type=F32)


def hbm(shape, dtype):
    return pltpu.HBM(shape, dtype)


def vmem_specs(count):
    return [pl.BlockSpec(memory_space=pltpu.VMEM)] * count


def row_values():
    return lax.broadcasted_iota(jnp.int32, (256, LANES), 0).astype(F32).astype(BF16)


def counts_of(index_ref, length_ref, group, values):
    lanes = slice(group * LANES, (group + 1) * LANES)
    length = length_ref[0:1, lanes]
    one, none = jnp.ones((256, LANES), BF16), jnp.zeros((256, LANES), BF16)
    counts = none
    for slot in range(4):
        ids = jnp.where(slot < length, index_ref[0, slot : slot + 1, lanes], -1).astype(F32)
        ids = jnp.broadcast_to(ids, (16, LANES)).astype(BF16)
        counts = counts + jnp.where(jnp.concatenate([ids] * 16, axis=0) == values, one, none)
    return counts


def pool_kernel(index_ref, length_ref, rows_ref, out_ref):
    values = row_values()
    low = low_lanes(HALF)
    right = jnp.concatenate([rows_ref[0], rows_ref[0]], axis=0)
    for group in range(STEP):
        counts = counts_of(index_ref, length_ref, group, values)
        pooled = lax.dot_general(
            counts, right, (((0,), (1,)), ((), ())), preferred_element_type=F32
        )
        pooled = jnp.where(low, pooled[0:HALF], pooled[HALF:LANES]).astype(BF16)
        for peer in range(4):
            out_ref[peer, group] = pooled[peer * ROWS : (peer + 1) * ROWS]


def in_hbm(*arrays):
    return [pltpu.with_memory_space_constraint(x, pltpu.HBM) for x in arrays]


def pool(pool_index, bag_length, rows):
    return pl.pallas_call(
        pool_kernel,
        grid=(TAB // STEP,),
        in_specs=[
            pl.BlockSpec((1, 4, STEP * LANES), lambda i: (0, 0, i)),
            pl.BlockSpec((1, STEP * LANES), lambda i: (0, i)),
            pl.BlockSpec((1, HALF, 256), lambda i: (0, 0, 0)),
        ],
        out_specs=pl.BlockSpec((4, STEP, ROWS, LANES), lambda i: (0, i, 0, 0)),
        out_shape=hbm((4, TAB, ROWS, LANES), BF16),
        compiler_params=pltpu.CompilerParams(vmem_limit_bytes=12 << 20),
        name="pool",
    )(*in_hbm(pool_index, bag_length, rows))


def packed_bottom(mine_ref):
    low = low_lanes(ROWS)
    tiles = []
    for pair in range(2):
        lanes = slice(pair * LANES, (pair + 1) * LANES)
        first, second = mine_ref[0:ROWS, lanes], mine_ref[ROWS : 2 * ROWS, lanes]
        tiles.append(jnp.where(low, first, turned(second, HALF)))
        tiles.append(jnp.where(low, turned(first, HALF), second))
    return jnp.concatenate(tiles, axis=1)


def interact_kernel(slot_ref, arrived_ref, mine_ref, label_ref, out_ref, vectors_ref, spaced, gram, edge):
    def place(table, carry):
        start = pl.multiple_of(slot_ref[table] * APART, 8)
        for part in range(4):
            spaced[part, pl.ds(start, ROWS), :] = arrived_ref[part, table].astype(F32)
        return carry

    lax.fori_loop(0, TAB, place, 0, unroll=8)
    bottom = packed_bottom(mine_ref)
    low = jnp.concatenate([low_lanes(TAB)] * 4, axis=1)
    first = jnp.where(low, 1.0, 0.0).astype(BF16)
    second = jnp.where(low, 0.0, 1.0).astype(BF16)
    for row in range(ROWS):
        vectors = jnp.concatenate(
            [spaced[part, pl.ds(row, TAB, stride=APART), :] for part in range(4)], axis=1
        )
        narrow = vectors.astype(BF16)
        vectors_ref[row] = narrow
        right = jnp.concatenate([narrow * first, narrow * second], axis=0)
        extra = jnp.broadcast_to(bottom[row : row + 1], (ROWS, 512)).astype(BF16)
        product = dot_t(jnp.concatenate([narrow, extra], axis=0), right)
        gram[pl.ds(row, TAB, stride=APART), :] = product[0:TAB]
        edge[row : row + 1, :] = product[TAB : TAB + 1]

    lane = lane_iota(ROWS)
    for half in range(2):
        where = slice(half * ROWS, (half + 1) * ROWS)
        out_ref[where, 0:EMB] = mine_ref[where, :].astype(BF16)
        tile, filled = EMB // LANES, jnp.zeros((ROWS, LANES), F32)
        for row, start, count, spot in pieces():
            source = edge[...] if row < 0 else gram[row * APART : row * APART + ROWS, :]
            moved = turned(source, spot - start - half * HALF)
            for at, first, _ in parts_of(spot, count):
                if at != tile:
                    out_ref[where, tile * LANES : (tile + 1) * LANES] = filled.astype(BF16)
                    tile, filled = at, moved
                filled = moved if first == 0 else jnp.where(lane >= first, moved, filled)
        filled = jnp.where(lane < FEAT % LANES, filled, jnp.where(lane == LABEL_LANE, label_ref[where, :], 0.0))
        out_ref[where, tile * LANES : (tile + 1) * LANES] = filled.astype(BF16)


def interact(table_slot, arrived, mine, labels):
    return pl.pallas_call(
        interact_kernel,
        in_specs=[
            pl.BlockSpec(memory_space=pltpu.SMEM),
            *vmem_specs(3),
        ],
        out_specs=[pl.BlockSpec(memory_space=pltpu.VMEM)] * 2,
        out_shape=[
            jax.ShapeDtypeStruct((2 * ROWS, WIDE), BF16),
            hbm((ROWS, TAB, 512), BF16),
        ],
        scratch_shapes=[
            pltpu.VMEM((4, TAB * APART, LANES), F32),
            pltpu.VMEM((TAB * APART, LANES), F32),
            pltpu.VMEM((ROWS, LANES), F32),
        ],
        compiler_params=pltpu.CompilerParams(vmem_limit_bytes=16 << 20),
        name="interact",
    )(table_slot, arrived, mine, labels)


def top_kernel(
    f0, f1, f2, f3, weight_ref, out_weight_ref,
    all_ref, z0, z1, z2, z3, partial_ref, delta_ref, hidden_ref,
):
    for part, ref in enumerate((f0, f1, f2, f3)):
        all_ref[part * 32 : (part + 1) * 32, :] = ref[...]
    weight = weight_ref[...]
    pre = jnp.dot(all_ref[:, 0:FEAT], weight, preferred_element_type=F32)
    sigma = jax.nn.sigmoid(pre)
    hidden = (pre * sigma).astype(BF16)
    slope = sigma * (1.0 + pre * (1.0 - sigma))
    out_weight = out_weight_ref[0:1, :]
    delta = (out_weight * slope).astype(BF16)
    hidden_ref[...] = hidden
    delta_ref[...] = delta
    partial = dot_t(jnp.broadcast_to(out_weight, (16, 512)).astype(BF16), hidden)[0:8]
    for place in range(8):
        partial_ref[place] = partial
    z = dot_t(delta, weight).astype(BF16)
    for part, ref in enumerate((z0, z1, z2, z3)):
        ref[:, 0:FEAT] = z[part * 32 : (part + 1) * 32]
        ref[:, FEAT:WIDE] = jnp.zeros((32, WIDE - FEAT), BF16)


def top(parts, top_weight, out_weight):
    return pl.pallas_call(
        top_kernel,
        in_specs=vmem_specs(6),
        out_specs=vmem_specs(8),
        out_shape=[hbm((128, WIDE), BF16), hbm((32, WIDE), BF16)]
        + [jax.ShapeDtypeStruct((32, WIDE), BF16)] * 3
        + [
            jax.ShapeDtypeStruct((8, 8, LANES), F32),
            hbm((128, 512), BF16),
            hbm((128, 512), BF16),
        ],
        compiler_params=pltpu.CompilerParams(vmem_limit_bytes=24 << 20),
        name="top",
    )(*parts, top_weight, out_weight)


def own_logits(even, r0, up1, down1, up2, down2):
    return (r0 + turned(up1, -32)) + (turned(down1, -64) + turned(jnp.where(even, up2, down2), -96))


def weight_grad_kernel(
    place_ref, partial_ref, all_ref, delta_ref, hidden_ref, own_ref, other_ref, grad,
):
    even = place_ref[1] == 0
    r0, up1, down1, up2, down2, far = (partial_ref[place_ref[2 + i]] for i in range(6))

    def at(x, slot, to):
        return turned(x, 32 * (to - slot))

    own = own_logits(even, r0, up1, down1, up2, down2)
    below = at(down1, 0, 1) + r0 + at(down2, 2, 1) + at(jnp.where(even, far, up1), 3, 1)
    above = at(up1, 0, 2) + at(up2, 1, 2) + r0 + at(jnp.where(even, down1, far), 3, 2)
    across = r0 + jnp.where(
        even,
        at(down2, 0, 3) + at(down1, 1, 3) + at(far, 2, 3),
        at(up2, 0, 3) + at(far, 1, 3) + at(up1, 2, 3),
    )
    block = lane_iota(8) // 32
    logits = jnp.where(block == 0, own, jnp.where(block == 1, below, jnp.where(block == 2, above, across)))
    tile = all_ref[:, WIDE - LANES : WIDE].astype(F32)
    labels = jnp.sum(jnp.where(lane_iota(128) == LABEL_LANE, tile, 0.0), axis=1, keepdims=True)
    column = (jax.nn.sigmoid(logits.T[:, 0:1]) - labels) * (1.0 / 128.0)
    delta = (delta_ref[...].astype(F32) * column).astype(BF16)
    last = WIDE - LANES
    grad[:, 0:last] = lax.dot_general(
        delta, all_ref[:, 0:last], (((0,), (0,)), ((), ())), preferred_element_type=F32
    )
    lane = lane_iota(128)
    coarse = column.astype(BF16).astype(F32)
    spots = jnp.where(lane == 32, coarse, jnp.where(lane == 33, column - coarse, 0.0)).astype(BF16)
    grad[:, last:WIDE] = lax.dot_general(
        jnp.concatenate([delta, hidden_ref[...]], axis=0),
        jnp.concatenate([all_ref[:, last:WIDE], spots], axis=0),
        (((0,), (0,)), ((), ())),
        preferred_element_type=F32,
    )
    core = place_ref[0]
    for x in range(4):
        for y in range(4):
            for ref, which in ((own_ref, core), (other_ref, 1 - core)):
                both = []
                for z in range(2):
                    first = pl.multiple_of((((x * 2 + z) * 4 + y) * 2 + which) * 8, 8)
                    both.append(grad[pl.ds(first, 8), :])
                ref[x * 4 + y] = jnp.concatenate(both, axis=0).astype(BF16)


def weight_grad(place, partials, features, delta, hidden):
    return pl.pallas_call(
        weight_grad_kernel,
        in_specs=[pl.BlockSpec(memory_space=pltpu.SMEM)] + vmem_specs(4),
        out_specs=vmem_specs(2),
        out_shape=[
            hbm((16, 16, WIDE), BF16),
            jax.ShapeDtypeStruct((16, 16, WIDE), BF16),
        ],
        scratch_shapes=[pltpu.VMEM((512, WIDE), F32)],
        compiler_params=pltpu.CompilerParams(vmem_limit_bytes=32 << 20),
        name="weight_grad",
    )(place, partials, *in_hbm(features, delta, hidden))


def spread_kernel(
    slot_ref, place_ref, z0, z1, z2, z3, partial_ref, label_ref, vectors_ref, mine_ref,
    slope_ref, dense_ref, back_ref, bottom_ref, logit_ref, dfeat, dpairs, upper, edge, dvec, dedge,
):
    logits = own_logits(place_ref[1] == 0, *(partial_ref[place_ref[2 + i]] for i in range(5)))
    logit_ref[...] = logits
    labels = jnp.sum(jnp.where(lane_iota(32) == LABEL_LANE, label_ref[...], 0.0), axis=1, keepdims=True)
    column = (jax.nn.sigmoid(logits.T[0:32, 0:1]) - labels) * (1.0 / 128.0)
    summed = z0[...].astype(F32) + z1[...].astype(F32) + z2[...].astype(F32) + z3[...].astype(F32)
    summed = summed * column
    dfeat[...] = summed[:, 0:EMB]
    dpairs[...] = summed.astype(BF16).astype(F32)
    lane = lane_iota(ROWS)
    none = jnp.zeros((ROWS, LANES), F32)
    for row, start, count, spot in pieces():
        filled = none
        for half in range(2):
            for at, first, _ in parts_of(spot, count):
                source = dpairs[half * ROWS : (half + 1) * ROWS, at * LANES : (at + 1) * LANES]
                moved = turned(source, start + half * HALF - spot)
                begin = first + start + half * HALF - spot + at * LANES
                filled = jnp.where(lane >= begin, moved, filled)
            if half == 0 and row >= 0:
                filled = jnp.where(lane >= HALF, 0.0, filled)
        if row < 0:
            edge[...] = filled
        else:
            upper[row * APART : row * APART + ROWS, :] = filled
    upper[(TAB - 1) * APART : (TAB - 1) * APART + ROWS, :] = jnp.zeros((ROWS, LANES), F32)
    bottom = packed_bottom(mine_ref)
    low = low_lanes(TAB)
    low_wide = jnp.concatenate([low] * 4, axis=1)
    low_factor = jnp.where(low_wide, 1.0, 0.0).astype(BF16)
    high_factor = jnp.where(low_wide, 0.0, 1.0).astype(BF16)
    low_few = jnp.concatenate([low_lanes(16)] * 4, axis=1)
    top_row = lax.broadcasted_iota(jnp.int32, (16, 512), 0) == 0
    low_own = jnp.where(top_row & low_few, 1.0, 0.0).astype(BF16)
    high_own = jnp.where(top_row & ~low_few, 1.0, 0.0).astype(BF16)
    empty = jnp.zeros((48, 512), BF16)
    for row in range(ROWS):
        half = upper[pl.ds(row, TAB, stride=APART), :]
        zeroth = jnp.broadcast_to(edge[row : row + 1, :], (TAB, LANES))
        flipped = jnp.concatenate([half, zeroth], axis=0).T
        first, second = flipped[0:TAB], turned(flipped[TAB : 2 * TAB], HALF)
        whole_matrix = half + jnp.where(low, first, second)
        edges = jnp.where(low, second, first)
        left = jnp.concatenate(
            [
                jnp.concatenate([whole_matrix, edges], axis=1),
                jnp.concatenate([zeroth[0:16], jnp.zeros((16, LANES), F32)], axis=1),
            ],
            axis=0,
        ).astype(BF16)
        vectors = vectors_ref[row]
        own = jnp.broadcast_to(bottom[row : row + 1], (16, 512)).astype(BF16)
        right = jnp.concatenate(
            [vectors * low_factor, vectors * high_factor, own * high_own, empty, own * low_own, empty], axis=0
        )
        product = jnp.dot(left, right, preferred_element_type=F32)
        for part in range(4):
            lanes = slice(part * LANES, (part + 1) * LANES)
            dvec[part, pl.ds(row, TAB, stride=APART), :] = product[0:TAB, lanes]
        dedge[row : row + 1, :] = product[TAB : TAB + 1]

    def place(table, carry):
        start = pl.multiple_of(slot_ref[table] * APART, 8)
        for part in range(4):
            back_ref[part, table] = dvec[part, pl.ds(start, ROWS), :].astype(BF16)
        return carry

    lax.fori_loop(0, TAB, place, 0, unroll=8)
    low = low_lanes(ROWS)
    tiles = [dedge[:, part * LANES : (part + 1) * LANES] for part in range(4)]
    own_rows = [
        jnp.concatenate(
            [jnp.where(low, tiles[2 * p], turned(tiles[2 * p + 1], HALF)) for p in range(2)], axis=1
        ),
        jnp.concatenate(
            [jnp.where(low, turned(tiles[2 * p], HALF), tiles[2 * p + 1]) for p in range(2)], axis=1
        ),
    ]
    dbottom = (dfeat[...] + jnp.concatenate(own_rows, axis=0)) * slope_ref[...]
    bottom_ref[...] = lax.dot_general(
        dense_ref[...],
        dbottom,
        (((0,), (0,)), ((), ())),
        precision=lax.Precision.HIGHEST,
        preferred_element_type=F32,
    )


def spread(table_slot, place, zs, partials, labels, vectors, mine, slope, dense):
    return pl.pallas_call(
        spread_kernel,
        in_specs=[pl.BlockSpec(memory_space=pltpu.SMEM)] * 2 + vmem_specs(10),
        out_specs=vmem_specs(3),
        out_shape=[
            hbm((4, TAB, ROWS, LANES), BF16),
            jax.ShapeDtypeStruct((16, EMB), F32),
            jax.ShapeDtypeStruct((8, LANES), F32),
        ],
        scratch_shapes=[
            pltpu.VMEM((2 * ROWS, EMB), F32),
            pltpu.VMEM((2 * ROWS, WIDE), F32),
            pltpu.VMEM((TAB * APART, LANES), F32),
            pltpu.VMEM((ROWS, LANES), F32),
            pltpu.VMEM((4, TAB * APART, LANES), F32),
            pltpu.VMEM((ROWS, 512), F32),
        ],
        compiler_params=pltpu.CompilerParams(vmem_limit_bytes=16 << 20),
        name="spread",
    )(table_slot, place, *zs, partials, labels, *in_hbm(vectors), mine, slope, dense)


def pack_kernel(place_ref, own_ref, other_ref, bottom_ref, keep_ref, s1, s2, s3, bottom_own_ref):
    high = bottom_ref[...].astype(BF16)
    low = (bottom_ref[...] - high.astype(F32)).astype(BF16)
    bottom_own_ref[...] = high.astype(F32) + low.astype(F32)
    tile = jnp.concatenate([v[:, p : p + LANES] for v in (high, low) for p in (0, LANES)], axis=0)
    for away, ref in enumerate((keep_ref, s1, s2, s3)):
        first = ((place_ref[8] + away) & 3) * 4
        for y in range(4):
            rows = slice(y * 16, (y + 1) * 16)
            total = own_ref[first + y].astype(F32) + other_ref[first + y].astype(F32)
            ref[rows, 0:WIDE] = total.astype(ref.dtype)
        if away:
            ref[:, WIDE:] = tile


def pack(place, own, other, bottom):
    return pl.pallas_call(
        pack_kernel,
        in_specs=[pl.BlockSpec(memory_space=pltpu.SMEM)] + vmem_specs(3),
        out_specs=vmem_specs(5),
        out_shape=[hbm((64, WIDE), BF16)]
        + [jax.ShapeDtypeStruct((64, WIDE + LANES), BF16)] * 3
        + [jax.ShapeDtypeStruct((16, EMB), F32)],
        compiler_params=pltpu.CompilerParams(vmem_limit_bytes=16 << 20),
        name="pack",
    )(place, *in_hbm(own), other, bottom)


def count_kernel(index_ref, length_ref, out_ref):
    values = row_values()
    for group in range(STEP):
        out_ref[:, group * LANES : (group + 1) * LANES] = counts_of(index_ref, length_ref, group, values)


def count(pool_index, bag_length):
    return pl.pallas_call(
        count_kernel,
        grid=(TAB // STEP,),
        in_specs=[
            pl.BlockSpec((1, 4, STEP * LANES), lambda i: (0, 0, i)),
            pl.BlockSpec((1, STEP * LANES), lambda i: (0, i)),
        ],
        out_specs=pl.BlockSpec((256, STEP * LANES), lambda i: (0, i)),
        out_shape=hbm((256, TAB * LANES), BF16),
        compiler_params=pltpu.CompilerParams(vmem_limit_bytes=12 << 20),
        name="count",
    )(*in_hbm(pool_index, bag_length))


def row_grad_kernel(count_ref, back_ref, out_ref, total):
    step = pl.program_id(0)

    @pl.when(step == 0)
    def _():
        total[...] = jnp.zeros_like(total)

    low = low_lanes(HALF)
    first = jnp.where(low, 1.0, 0.0).astype(BF16)
    second = jnp.where(low, 0.0, 1.0).astype(BF16)
    moved = []
    for group in range(GRAD_STEP):
        rows = jnp.concatenate([back_ref[peer, group] for peer in range(4)], axis=0)
        moved += [rows * first, rows * second]
    total[...] += jnp.dot(count_ref[...], jnp.concatenate(moved, axis=0), preferred_element_type=F32)

    @pl.when(step == pl.num_programs(0) - 1)
    def _():
        flipped = total[...].T
        out_ref[0] = flipped[0:HALF] + flipped[HALF:LANES]


def row_grad(counts, back):
    return pl.pallas_call(
        row_grad_kernel,
        grid=(TAB // GRAD_STEP,),
        in_specs=[
            pl.BlockSpec((256, GRAD_STEP * LANES), lambda i: (0, i)),
            pl.BlockSpec((4, GRAD_STEP, ROWS, LANES), lambda i: (0, i, 0, 0)),
        ],
        out_specs=pl.BlockSpec((1, HALF, 256), lambda i: (0, 0, 0)),
        out_shape=jax.ShapeDtypeStruct((1, HALF, 256), F32),
        scratch_shapes=[
            pltpu.VMEM((256, LANES), F32),
        ],
        compiler_params=pltpu.CompilerParams(vmem_limit_bytes=16 << 20),
        name="row_grad",
    )(*in_hbm(counts), back)


def shifted(x, axis, shift):
    size = lax.axis_size(axis)
    return lax.ppermute(x, axis, [(i, (i + shift) % size) for i in range(size)])


def ring_sent(x, moves):
    def spot(place):
        return place % 4 * 2 + place % 8 // 4

    pairs = [(spot(p), spot(p + moves(p))) for p in range(8)]
    return lax.ppermute(x, ("col", "grp_1"), pairs)


def exchange_all(x):
    flat = x.reshape(4 * TAB, ROWS, LANES)
    flat = lax.all_to_all(flat, COL_GRP, split_axis=0, concat_axis=0, tiled=True)
    return flat.reshape(4, TAB, ROWS, LANES)


def summed_over(x, axis):
    if lax.axis_size(axis) == 2:
        return x + shifted(x, axis, 1)
    others = [shifted(x, axis, shift) for shift in (1, 2, 3)]
    return (x + others[1]) + (others[0] + others[2])


def split(x):
    high = x.astype(BF16)
    return high, (x - high.astype(F32)).astype(BF16)


def reduced_to(x, axis, shared=None):
    me = lax.axis_index(axis)
    size = lax.axis_size(axis)
    total = lax.dynamic_index_in_dim(x, me, 0, keepdims=False).astype(F32)
    rows, width = total.shape
    if shared is not None:
        high, low = split(shared)
        own = high.astype(F32) + low.astype(F32)
        cuts = [v[r : r + rows] for v in (high, low) for r in range(0, shared.shape[0], rows)]
    others = []
    for shift in range(1, size):
        block = lax.dynamic_index_in_dim(x, (me + shift) % size, 0, keepdims=False).astype(BF16)
        if shared is not None:
            block = jnp.concatenate([block, *cuts], axis=1)
        block = shifted(block, axis, shift).astype(F32)
        total = total + block[:, 0:width]
        if shared is not None:
            wide = shared.shape[1]
            parts = [block[:, p : p + wide] for p in range(width, block.shape[1], wide)]
            half = len(parts) // 2
            others.append(jnp.concatenate([a + b for a, b in zip(parts[:half], parts[half:])], axis=0))
    if shared is None:
        return total
    if size == 2:
        return total, own + others[0]
    return total, (own + others[1]) + (others[0] + others[2])


def silu_slope(values):
    sigma = jax.nn.sigmoid(values)
    return sigma * (1.0 + values * (1.0 - sigma))


def step(
    table_rows,
    pool_index,
    bag_length,
    table_slot,
    dense_input,
    bottom_weight,
    top_weight,
    out_weight,
    labels,
):
    me, core = lax.axis_index("col"), lax.axis_index("grp_3")
    rows = jnp.transpose(table_rows, (0, 2, 1))
    pooled = pool(pool_index, bag_length, rows)
    arrived = exchange_all(pooled)

    dense_mine = lax.dynamic_index_in_dim(
        dense_input.reshape(2, 4, ROWS, -1), me, 1, keepdims=False
    ).reshape(2 * ROWS, -1)
    mine_pre = jnp.dot(dense_mine, bottom_weight, preferred_element_type=F32)
    mine = jax.nn.silu(mine_pre).astype(BF16).astype(F32)
    mine_slope = silu_slope(mine_pre)
    dense_wide = jnp.pad(dense_mine.astype(F32), ((0, 0), (0, 16 - dense_mine.shape[1])))
    labels_mine = lax.dynamic_index_in_dim(labels.reshape(2, 4, ROWS), me, 1, keepdims=False)
    labels_mine = jnp.broadcast_to(labels_mine.astype(F32).reshape(2 * ROWS, 1), (2 * ROWS, LANES))
    spot = lax.axis_index("grp_1") * 4 + me
    near = [spot, spot + 1, spot - 1, spot + 2, spot - 2, jnp.where(me % 2 == 0, spot - 3, spot + 3)]
    near = [p % 4 * 2 + p % 8 // 4 for p in near]
    place = jnp.stack([core, me % 2, *near, lax.axis_index("grp_0")]).astype(jnp.int32)
    out_weight_row = out_weight.astype(F32).reshape(1, -1)

    counts = count(pool_index, bag_length)
    part, vectors = interact(table_slot, arrived, mine, labels_mine)
    parts = [
        part,
        ring_sent(part, lambda p: 1),
        ring_sent(part, lambda p: -1),
        ring_sent(part, lambda p: -2 if p % 2 else 2),
    ]
    features, *zs, partial, delta, hidden = top(parts, top_weight, out_weight_row)
    zs = [
        zs[0],
        ring_sent(zs[1], lambda p: -1),
        ring_sent(zs[2], lambda p: 1),
        ring_sent(zs[3], lambda p: 2 if p % 2 else -2),
    ]
    partials = lax.all_to_all(partial, ("col", "grp_1"), split_axis=0, concat_axis=0, tiled=True)
    own, other = weight_grad(place, partials, features, delta, hidden)
    back, bottom, logits_mine = spread(
        table_slot, place, zs, partials, labels_mine, vectors, mine, mine_slope, dense_wide
    )
    returned = exchange_all(back)
    grad_rows = jnp.transpose(row_grad(counts, returned), (0, 2, 1))

    other = shifted(other, "grp_3", 1)
    grad, *blocks, bottom = pack(place, own, other, bottom)
    grad = grad.astype(F32)
    sums = []
    for away in (1, 2, 3):
        block = shifted(blocks[away - 1], "grp_0", away).astype(F32)
        grad = grad + block[:, 0:WIDE]
        tile = block[0:32, WIDE:] + block[32:64, WIDE:]
        sums.append(jnp.concatenate([tile[0:16], tile[16:32]], axis=1))
    grad = grad.reshape(4, 16, WIDE)
    bottom = summed_over((bottom + sums[1]) + (sums[0] + sums[2]), "grp_3")
    grad, bottom = reduced_to(grad, "grp_2", bottom)
    grad, bottom = reduced_to(grad.reshape(2, 8, WIDE), "grp_1", bottom)
    grad_top = jnp.transpose(grad[:, 0:FEAT])
    grad_out = grad[:, FEAT] + grad[:, FEAT + 1]
    spots = jnp.tile(logits_mine[0:1, 0:32], (1, EMB // 32))
    row = lax.broadcasted_iota(jnp.int32, bottom.shape, 0)
    lane = lax.broadcasted_iota(jnp.int32, bottom.shape, 1)
    spare = bottom_weight.shape[0]
    bottom = jnp.where(row == spare, jnp.where(lane // 32 == me, spots, 0.0), bottom)
    bottom = summed_over(bottom, "col")
    grad_bottom = bottom[0:spare]
    logits = jnp.transpose(bottom[spare, 0:LANES].reshape(4, 2, ROWS), (1, 0, 2)).reshape(LANES)
    return (logits, grad_top, grad_out, grad_bottom, grad_rows)


def solution(mesh):
    torus = Mesh(
        mesh.devices.reshape(mesh.shape["col"], 4, 2, 4, 2),
        ("col", "grp_0", "grp_1", "grp_2", "grp_3"),
    )
    return jax.shard_map(
        step,
        mesh=torus,
        in_specs=(
            P(GRP, None, "col"),
            P(GRP, None, None),
            P(GRP, None),
            P(),
            P(GRP, None),
            P(),
            P(None, "col"),
            P("col"),
            P(GRP),
        ),
        out_specs=(P(GRP), P(None, COL_GRP), P(COL_GRP), P(), P(GRP, None, "col")),
        check_vma=False,
    )
```
